512 devices in a mesh: dp: 64 (over y_lo, z, core), tensor: 8 (over y_hi, x).
Axes of the slice: x: 4, y: 8 (y_hi: 2, y_lo: 4; y = y_hi * 4 + y_lo), z: 8, core: 2. Of those that a mesh axis runs over, the one named last changes fastest.
Arguments:
- hidden_rows: bfloat16 [4096, 16384], P('dp', 'tensor')
- norm_gain: float32 [16384], P('tensor'), may hold values from 0.5 to 1.5
- key_weight: bfloat16 [512, 16384], P('dp', 'tensor'), may hold values from -0.046875 to 0.046875
- cotangent: bfloat16 [64, 128, 512], P('dp'), may hold values from -16 to 16
- accepted_counts: int32 [64], P('dp'), may hold values from 16 to 64, as said below
- destination: int32 [4096], P('dp'), may hold values from 0 to 63, as said below
Outputs:
- keys: bfloat16 [64, 128, 512], P('dp')
- key_weight_grad: float32 [512, 16384], P('dp', 'tensor')
- gain_grad: float32 [16384], P('tensor')
The draws below stay inside these ranges and needn't reach their ends.
Inputs may be any that keep to these rules, and one draw needn't show every extreme that they name: `accepted_counts`: rows 0 to the count minus 1 of a replica are accepted; in every draw one replica accepts all its rows and another a quarter of them. `destination`: among one replica's 64 rows no shard is named more than 2 times; in every draw one shard is named exactly 2 times by every replica, all within the first quarter of that replica's rows.
All inputs are finite; a program needn't handle non-finite values.
Results may differ from the reference program's by a relative error of at most 0.0051.
Values may be sent and summed in bfloat16 or wider, within the bound.
A program may use at most 64 MiB of HBM per device.

```python
import math
import jax
import jax.numpy as jnp
from jax import lax

D = 16384
KVW = 512
ROWS = 64
DATA_COPIES = 64
CAP = 2
SLOTS = 128
TOTAL_ROWS = 4096


def draw_hidden_rows(key, part):
    key_noise, key_row, key_column = jax.random.split(key, 3)
    position = jnp.arange(D, dtype=jnp.float32) / D
    noise_base = jnp.clip(jax.random.normal(key_noise, (TOTAL_ROWS, D), jnp.float32), -6.0, 6.0)
    rising = jnp.exp(position * (0.5 * math.log(4.0)))
    row_scale = jnp.exp(jax.random.uniform(key_row, (TOTAL_ROWS, 1), jnp.float32, 0.0, math.log(10.0)))
    column_scale = jnp.exp(jax.random.uniform(key_column, (D,), jnp.float32, 0.0, math.log(10.0)))
    return (noise_base * row_scale * (column_scale * rising)[None, :]).astype(jnp.bfloat16)


def draw_accepted_counts(key, part):
    key_values, key_top, key_low = jax.random.split(key, 3)
    counted = jax.random.randint(key_values, (DATA_COPIES,), ROWS // 4, ROWS + 1)
    top_replica = jax.random.randint(key_top, (), 0, DATA_COPIES)
    low_replica = (top_replica + 1 + jax.random.randint(key_low, (), 0, DATA_COPIES - 1)) % DATA_COPIES
    return counted.at[top_replica].set(ROWS).at[low_replica].set(ROWS // 4).astype(jnp.int32)


def draw_destination(key, part):
    busiest_key, extra_token_key, rows_key_seed = jax.random.split(key, 3)
    position_count = DATA_COPIES * CAP
    busiest_partition = jax.random.randint(busiest_key, (), 0, DATA_COPIES)
    partition_index = jnp.arange(DATA_COPIES, dtype=jnp.int32)
    extra_token = jax.random.randint(extra_token_key, (DATA_COPIES,), 0, 4)
    extra_token = jnp.where(partition_index == busiest_partition, 8, extra_token)
    position_index = jnp.arange(position_count, dtype=jnp.int32)
    position_holder = position_index // CAP
    row_ids = jnp.arange(ROWS, dtype=jnp.int32)

    def one_replica(replica):
        key_replica = jax.random.fold_in(rows_key_seed, replica)
        key_pick, key_rank, key_place = jax.random.split(key_replica, 3)
        random_selection = jax.random.randint(key_pick, (position_count,), 0, 16384)
        priority_rating = (extra_token[position_holder] * 16384 + random_selection) * position_count + position_index
        chosen = lax.top_k(priority_rating, ROWS)[1]
        target = chosen // CAP
        is_hot = target == busiest_partition
        rank_key = jnp.where(is_hot, 16384, jax.random.randint(key_rank, (ROWS,), 0, 16384)) * ROWS + row_ids
        ranking = jnp.argsort(jnp.argsort(rank_key))
        early = is_hot | (ranking < ROWS // 4 - CAP)
        place_key = jnp.where(early, 0, 16384) + jax.random.randint(key_place, (ROWS,), 0, 16384)
        place_key = place_key * ROWS + row_ids
        return target[jnp.argsort(place_key)]
    return jax.vmap(one_replica)(partition_index).reshape(-1).astype(jnp.int32)


def with_spikes(result, rng, source, target, parts, factor):
    def block_of(dim):
        return (jnp.arange(result.shape[dim]) // (result.shape[dim] // parts)).reshape((-1,) + (1,) * (result.ndim - 1 - dim))

    first = jax.random.permutation(rng, parts)[block_of(target)]
    second = (block_of(target) + parts // 2) % parts
    return jnp.where((block_of(source) == first) | (block_of(source) == second), factor * result, result)


def level_of(stream_key, dims, shards, least, top_value):
    def one(dim, parts):
        steps = jax.random.uniform(jax.random.fold_in(jax.random.fold_in(stream_key, 6), dim), (parts,), jnp.float32, least / len(shards), top_value / len(shards))
        return jnp.repeat(jnp.exp(steps), dims[dim] // parts).reshape((-1,) + (1,) * (len(dims) - dim - 1))

    factor_of = one(*shards[0])
    for cut in shards[1:]:
        factor_of = factor_of * one(*cut)
    return factor_of


def bell_draw(stream_key, extent, deviation, reach, cuts=(), held_as=jnp.bfloat16):
    gain = level_of(stream_key, extent, cuts, -0.22, 0.18) if cuts else 1.0
    array = jax.random.normal(stream_key, extent, jnp.float32) * deviation * gain
    return jnp.minimum(jnp.maximum(array, -reach), reach).astype(held_as)


def noise_with(stream_key, dims, scale, reach, cuts, heavy, held_as=jnp.bfloat16):
    entries = scale * jax.random.normal(stream_key, dims, jnp.float32)
    if cuts:
        entries = entries * level_of(stream_key, dims, cuts, -0.22, 0.18)
    return jnp.clip(with_spikes(entries, jax.random.fold_in(stream_key, 3), *heavy), -reach, reach).astype(held_as)


def setup_inputs(seed: int = 0) -> dict:
    splits = jax.random.split(jax.random.key(seed), 7)
    hidden_rows = draw_hidden_rows(jax.random.fold_in(splits[6], 71), 0)
    norm_gain = jnp.clip(1.0 + 0.1 * jax.random.normal(splits[1], (D,), jnp.float32), 0.5, 1.5)
    key_weight = bell_draw(splits[2], (KVW, D), D ** -0.5, 0.046875, ((0, 64), (1, 8)))
    cotangent = noise_with(splits[3], (DATA_COPIES, SLOTS, KVW), 1.0, 16.0, ((0, 64),), (0, 2, 64, 4.0))
    accepted_counts = draw_accepted_counts(jax.random.fold_in(splits[6], 71), 0)
    destination = draw_destination(jax.random.fold_in(splits[6], 71), 0)
    return dict(hidden_rows=hidden_rows, norm_gain=norm_gain, key_weight=key_weight, cotangent=cotangent, accepted_counts=accepted_counts, destination=destination)


EPSILON = 1e-05

def layout(dest_rows, count):
    row_total = dest_rows.shape[0]
    row_order = jnp.arange(row_total, dtype=jnp.int32)
    onehot = (dest_rows[:, None] == jnp.arange(DATA_COPIES, dtype=jnp.int32)[None, :]).astype(jnp.int32)
    before = jnp.cumsum(onehot, axis=0) - onehot
    slot_rank = lax.optimization_barrier(jnp.sum(before * onehot, axis=1)).astype(jnp.int32)
    return (row_order < count, slot_rank)

def reference(hidden_rows, norm_gain, key_weight, cotangent, accepted_counts, destination):
    factor = 1.0 / math.sqrt(TOTAL_ROWS)
    blocks = hidden_rows.reshape(DATA_COPIES, ROWS, D)
    targets = destination.reshape(DATA_COPIES, ROWS)

    def one_replica(running, inputs):
        grad_weight, grad_gain = running
        row_data, dest_rows, count, replica = inputs
        accepted, slot_rank = layout(dest_rows, count)
        row_values = jnp.where(accepted[:, None], row_data.astype(jnp.float32), jnp.float32(0.0))
        mean_square = lax.optimization_barrier(jnp.sum(row_values * row_values, axis=1)) / D
        normed = (row_values * lax.rsqrt(mean_square + EPSILON)[:, None] * norm_gain[None, :]).astype(jnp.bfloat16)
        row_keys = lax.dot_general(normed, key_weight, (((1,), (1,)), ((), ())), preferred_element_type=jnp.float32).astype(jnp.bfloat16)
        slot_column = (replica * CAP + slot_rank).astype(jnp.int32)
        row_cotangent = cotangent[dest_rows, slot_column]
        grad_weight = grad_weight + lax.dot_general(row_cotangent, normed, (((0,), (0,)), ((), ())), preferred_element_type=jnp.float32)
        backward = jnp.dot(row_cotangent, key_weight, preferred_element_type=jnp.float32)
        grad_gain = grad_gain + lax.optimization_barrier(jnp.sum(backward * normed.astype(jnp.float32), axis=0))
        return ((grad_weight, grad_gain), (row_keys, slot_column, accepted))
    start_state = (jnp.zeros((KVW, D), jnp.float32), jnp.zeros((D,), jnp.float32))
    replica_ids = jnp.arange(DATA_COPIES, dtype=jnp.int32)
    (grad_weight, grad_gain), (all_keys, columns, accepted_all) = lax.scan(one_replica, start_state, (blocks, targets, accepted_counts, replica_ids))
    target_shard = jnp.where(accepted_all, targets, DATA_COPIES).astype(jnp.int32)
    keys = jnp.zeros((DATA_COPIES, SLOTS, KVW), jnp.bfloat16)
    keys = keys.at[target_shard.reshape(-1), columns.reshape(-1)].set(all_keys.reshape(-1, KVW), mode='drop')
    return (keys, grad_weight * factor, grad_gain * factor / norm_gain)
```

```python
import functools
import math

import jax
import jax.numpy as jnp
from jax import lax
from jax.experimental import pallas as pl
from jax.experimental.pallas import tpu as pltpu
from jax.sharding import PartitionSpec as P

EPSILON = 1e-05
F32 = jnp.float32
BF16 = jnp.bfloat16
MESH = pl.DeviceIdType.MESH


def iota(shape, dim):
    return lax.broadcasted_iota(jnp.int32, shape, dim)


def onehot(cond):
    return jnp.where(cond, 1.0, 0.0).astype(BF16)


def kernel(
    dims,
    factor,
    hid,
    gain_ref,
    wsh,
    cot,
    count_ref,
    dest_ref,
    keys_out,
    gw_out,
    gg_out,
    hbuf,
    wown,
    wpart,
    wall,
    cotv,
    cot_a,
    cot_b1,
    cot_s,
    cot_b2,
    cot_r,
    sqb,
    sqc,
    norm,
    gf,
    gs,
    ra,
    rb,
    sa,
    sb,
    gy_s,
    gy_r,
    gc_s,
    gout,
    gz,
    gyb,
    gcb,
    k_part,
    kc_s,
    kc_r,
    kx_s,
    kx_r,
    kh_s,
    kh_r,
    kz_s,
    kz_r,
    ky_s,
    ky_r,
    kout,
    ssem,
    rsem,
    lsem,
):
    NY, NZ, NH, NX = dims
    NT = NH * NX
    dp = lax.axis_index("dp")
    t = lax.axis_index("tensor")
    c = lax.rem(dp, 2)
    z = lax.rem(lax.div(dp, 2), NZ)
    y = lax.div(dp, 2 * NZ)
    x = lax.rem(t, NX)
    h = lax.div(t, NX)
    rows = dest_ref.shape[1]
    slots = 2 * rows
    half = hbuf.shape[2]
    width = half * 2 * NT
    kvw = cotv.shape[1]
    qcols = kvw // NX
    sign = 1 - 2 * c
    LA, LB = NZ // 2, NZ // 2 - 1

    def at_dp(yy, zz, cc):
        return {"dp": (yy * NZ + zz) * 2 + cc}

    partner = at_dp(y, z, 1 - c)
    z_fwd = at_dp(y, lax.rem(z + sign + NZ, NZ), c)
    z_bwd = at_dp(y, lax.rem(z - sign + NZ, NZ), c)

    def zmod(v):
        return lax.rem(v + 2 * NZ, NZ)

    counter = [0]
    sends = []

    def remote(src, dst, dev):
        i = counter[0]
        counter[0] += 1
        d = pltpu.make_async_remote_copy(
            src_ref=src,
            dst_ref=dst,
            send_sem=ssem.at[i],
            recv_sem=rsem.at[i],
            device_id=dev,
            device_id_type=MESH,
        )
        d.start()
        sends.append(d)
        return d

    lcount = [0]

    def local(src, dst):
        i = lcount[0]
        lcount[0] += 1
        d = pltpu.make_async_copy(src, dst, lsem.at[i])
        d.start()
        return d

    own_cols = pl.ds(pl.multiple_of(c * half, half), half)
    other_cols = pl.ds(pl.multiple_of((1 - c) * half, half), half)

    barrier = pltpu.get_barrier_semaphore()
    peers = []
    for d in range(1, NZ):
        peers.append(at_dp(y, lax.rem(z + d, NZ), c))
    for dy in range(NY):
        for dc in range(2):
            if dy or dc:
                peers.append(at_dp(lax.rem(y + dy, NY), z, lax.rem(c + dc, 2)))
    for d in range(1, NT):
        peers.append({"tensor": lax.rem(t + d, NT)})
    for p in peers:
        pl.semaphore_signal(barrier, inc=1, device_id=p, device_id_type=MESH)

    l_cot = local(cot.at[0], cotv)
    l_w = local(wsh.at[:, own_cols], wown)
    l_h = local(hid.at[:, own_cols], hbuf.at[c])

    def perm_zy():
        b = iota((slots, slots), 1)
        bz = (b // 4) % NZ
        by = b // (4 * NZ)
        return onehot(iota((slots, slots), 0) == bz * (4 * NY) + by * 4 + b % 4)

    def perm_yz():
        b = iota((slots, slots), 1)
        bz = b // (4 * NY)
        byc = (b // 2) % (2 * NY)
        return onehot(iota((slots, slots), 0) == byc * (2 * NZ) + bz * 2 + b % 2)

    def perm_out():
        b = iota((slots, slots), 1)
        by = b // (4 * NZ)
        bc = (b // (2 * NZ)) % 2
        bz = (b // 2) % NZ
        return onehot(iota((slots, slots), 0) == by * (4 * NZ) + bz * 4 + bc * 2 + b % 2)

    def dot(a, b):
        return jnp.dot(a, b, preferred_element_type=F32)

    l_cot.wait()
    mixed = dot(perm_zy(), cotv[...]).astype(BF16)
    cot_a[...] = mixed.reshape(NZ, 4 * NY, kvw)

    pl.semaphore_wait(barrier, len(peers))

    r_w = remote(wsh.at[:, other_cols], wpart, partner)
    r_h = remote(hid.at[:, other_cols], hbuf.at[c], partner)

    def z_exchange(src, dst):
        return [
            remote(src.at[lax.rem(z + d, NZ)], dst.at[z], at_dp(y, lax.rem(z + d, NZ), c))
            for d in range(1, NZ)
        ]

    def yc_exchange(src, dst):
        out = []
        for dy in range(NY):
            for dc in range(2):
                if dy or dc:
                    yy, cc = lax.rem(y + dy, NY), lax.rem(c + dc, 2)
                    out.append(remote(src.at[yy * 2 + cc], dst.at[y * 2 + c], at_dp(yy, z, cc)))
        return out

    def recv(copies):
        for d in copies:
            d.wait_recv()

    r_cz = z_exchange(cot_a, cot_b1)
    cot_b1[pl.ds(z, 1)] = cot_a[pl.ds(z, 1)]

    l_w.wait()
    r_w.wait_recv()
    mine, theirs = wown[...].astype(F32), wpart[...].astype(F32)
    low = jnp.where(c == 0, mine, theirs)
    high = jnp.where(c == 0, theirs, mine)
    wall[pl.ds(y, 1), pl.ds(z, 1)] = (
        jnp.concatenate([low, high], axis=0).astype(BF16).reshape(1, 1, 2 * low.shape[0], half)
    )
    r_wy = [
        remote(wall.at[y, z], wall.at[y, z], at_dp(lax.rem(y + d, NY), z, c)) for d in range(1, NY)
    ]

    def w_send(step, d, fwd):
        yy = lax.rem(y - d + NY, NY)
        zz = zmod(z - (step - 1) * sign) if fwd else zmod(z + (step - 1) * sign)
        return remote(wall.at[yy, zz], wall.at[yy, zz], z_fwd if fwd else z_bwd)

    wa, wb = {}, {}

    def w_step(step, d):
        if step <= LA:
            wa[step, d] = w_send(step, d, True)
        if step <= LB:
            wb[step, d] = w_send(step, d, False)

    def w_recv(step, d):
        if step <= LA:
            wa[step, d].wait_recv()
        if step <= LB:
            wb[step, d].wait_recv()

    w_step(1, 0)

    l_h.wait()
    r_h.wait_recv()
    values = hbuf[...].astype(F32).reshape(2 * rows, half)
    sums = jnp.sum(values * values, axis=1, keepdims=True)
    eye2 = iota((2 * rows, 2 * rows), 0) == iota((2 * rows, 2 * rows), 1)
    sqb[pl.ds(t, 1)] = jnp.sum(jnp.where(eye2, sums, 0.0), axis=0, keepdims=True)[None]
    r_sq = [
        remote(sqb.at[t], sqb.at[t], {"tensor": lax.rem(t + d, NT)}) for d in range(1, NT)
    ]

    for d in range(1, NY):
        r_wy[d - 1].wait_recv()
        w_step(1, d)

    recv(r_cz)
    cot_s[...] = (
        dot(perm_yz(), cot_b1[...].reshape(slots, kvw)).astype(BF16).reshape(2 * NY, 2 * NZ, kvw)
    )
    r_cy = yc_exchange(cot_s, cot_b2)
    cot_b2[pl.ds(y * 2 + c, 1)] = cot_s[pl.ds(y * 2 + c, 1)]

    for d in range(NY):
        w_recv(1, d)
        w_step(2, d)

    drow = dest_ref[...]
    sq_shape = (rows, rows)
    eye = iota(sq_shape, 0) == iota(sq_shape, 1)
    dcol = jnp.sum(jnp.where(eye, drow.astype(F32), 0.0), axis=1, keepdims=True).astype(jnp.int32)
    same = dcol == drow
    rank_col = jnp.sum(
        jnp.where(same & (iota(sq_shape, 1) < iota(sq_shape, 0)), 1.0, 0.0), axis=1, keepdims=True
    ).astype(jnp.int32)
    rank_row = jnp.sum(
        jnp.where(same & (iota(sq_shape, 0) < iota(sq_shape, 1)), 1.0, 0.0), axis=0, keepdims=True
    ).astype(jnp.int32)
    count = count_ref[0]

    recv(r_sq)
    total = sqb[0]
    for i in range(1, NT):
        total = total + sqb[i]
    sqc[pl.ds(c, 1)] = total[None]
    r_sc = remote(sqc.at[c], sqc.at[c], partner)

    recv(r_cy)
    d_yc = (dcol // (2 * NZ)) * 2 + dcol % 2
    d_z = (dcol // 2) % NZ
    pos_col = d_yc * (2 * NZ) + d_z * 2 + rank_col
    pick = onehot(
        (iota((rows, slots), 1) == pos_col) & (iota((rows, slots), 0) < count)
    )
    cot_r[pl.ds(c, 1)] = dot(pick, cot_b2[...].reshape(slots, kvw)).astype(BF16)[None]
    r_cr = remote(cot_r.at[c], cot_r.at[c], partner)

    for d in range(NY):
        w_recv(2, d)
        w_step(3, d)

    r_sc.wait_recv()
    total = sqc[0] + sqc[1]
    scale = lax.rsqrt(total / width + EPSILON)
    scale_col = jnp.sum(jnp.where(eye2, scale, 0.0), axis=1, keepdims=True)
    gain_half = gain_ref[:, own_cols]
    norm[...] = (
        hbuf[...].astype(F32).reshape(2 * rows, half) * scale_col * gain_half
    ).astype(BF16)

    r_cr.wait_recv()
    cot2 = cot_r[...].reshape(2 * rows, kvw)
    kb = kvw // NY
    for yy in range(NY):
        part = lax.dot_general(
            cot2[:, yy * kb : (yy + 1) * kb],
            norm[...],
            (((0,), (0,)), ((), ())),
            preferred_element_type=F32,
        ).reshape(NZ, kb // NZ, half)
        gf[yy] = part
        gs[yy] = part.astype(BF16)

    for step in range(3, LA):
        for d in range(NY):
            w_recv(step, d)
            w_step(step + 1, d)

    ga, gb = {}, {}
    za1, zb1 = zmod(z + LA * sign), zmod(z - LB * sign)
    for yy in range(NY):
        ga[1, yy] = remote(gs.at[yy, za1], ra.at[0, yy], z_fwd)
        if LB:
            gb[1, yy] = remote(gs.at[yy, zb1], rb.at[0, yy], z_bwd)

    def g_step(step):
        for yy in range(NY):
            if step <= LA:
                ga[step - 1, yy].wait_recv()
                zz = zmod(z + (LA + 1 - step) * sign)
                own = gf[yy, pl.ds(zz, 1)][0]
                sa[step - 2, yy] = (ra[step - 2, yy].astype(F32) + own).astype(BF16)
                ga[step, yy] = remote(sa.at[step - 2, yy], ra.at[step - 1, yy], z_fwd)
            if step <= LB:
                gb[step - 1, yy].wait_recv()
                zz = zmod(z - (LB + 1 - step) * sign)
                own = gf[yy, pl.ds(zz, 1)][0]
                sb[step - 2, yy] = (rb[step - 2, yy].astype(F32) + own).astype(BF16)
                gb[step, yy] = remote(sb.at[step - 2, yy], rb.at[step - 1, yy], z_bwd)

    if LA > 2:
        for d in range(NY):
            w_recv(LA, d)

    for yy in range(NY):
        k_part[:, yy * kb : (yy + 1) * kb] = lax.dot_general(
            norm[...],
            wall[yy].reshape(kb, half),
            (((1,), (1,)), ((), ())),
            preferred_element_type=F32,
        )
    kc_s[...] = k_part[pl.ds(pl.multiple_of((1 - c) * rows, rows), rows), :]
    r_kc = remote(kc_s, kc_r, partner)

    gain_sum = jnp.zeros((1, half), F32)
    for yy in range(NY):
        gain_sum += jnp.sum(
            (gf[yy] * wall[yy].astype(F32)).reshape(kb, half), axis=0, keepdims=True
        )
    gz[pl.ds(z, 1)] = gain_sum[None]
    r_gz = [
        remote(gz.at[z], gz.at[z], at_dp(y, lax.rem(z + d, NZ), c)) for d in range(1, NZ)
    ]

    r_kc.wait_recv()
    own_k = k_part[pl.ds(pl.multiple_of(c * rows, rows), rows), :] + kc_r[...]
    for q in range(NX):
        kx_s[q] = own_k[:, q * qcols : (q + 1) * qcols].astype(BF16)
    kx_r[pl.ds(x, 1)] = kx_s[pl.ds(x, 1)]
    r_kx = []
    for d in range(1, NX):
        xx = lax.rem(x + d, NX)
        r_kx.append(remote(kx_s.at[xx], kx_r.at[x], {"tensor": h * NX + xx}))

    if LA >= 2:
        g_step(2)

    recv(r_kx)
    mine_k = kx_r[0].astype(F32)
    for q in range(1, NX):
        mine_k = mine_k + kx_r[q].astype(F32)
    if NH == 2:
        kh_s[...] = mine_k.astype(BF16)
        r_kh = remote(kh_s, kh_r, {"tensor": (1 - h) * NX + x})

    recv(r_gz)
    gain_sum = gz[0]
    for i in range(1, NZ):
        gain_sum = gain_sum + gz[i]
    gyb[pl.ds(y, 1)] = gain_sum[None]
    r_gy = [
        remote(gyb.at[y], gyb.at[y], at_dp(lax.rem(y + d, NY), z, c)) for d in range(1, NY)
    ]

    if LA >= 3:
        g_step(3)

    if NH == 2:
        r_kh.wait_recv()
        mine_k = kh_s[...].astype(F32) + kh_r[...].astype(F32)
    r_yc = (drow // (2 * NZ)) * 2 + drow % 2
    r_z = (drow // 2) % NZ
    pos_row = r_z * (4 * NY) + r_yc * 2 + rank_row
    place = onehot(
        (iota((slots, rows), 0) == pos_row) & (iota((slots, rows), 1) < count)
    )
    kz_s[...] = dot(place, mine_k.astype(BF16)).astype(BF16).reshape(NZ, 4 * NY, qcols)
    r_kz = z_exchange(kz_s, kz_r)
    kz_r[pl.ds(z, 1)] = kz_s[pl.ds(z, 1)]

    for step in range(4, LA + 1):
        g_step(step)

    recv(r_gy)
    gain_sum = gyb[0]
    for i in range(1, NY):
        gain_sum = gain_sum + gyb[i]
    gcb[pl.ds(c, 1)] = (gain_sum * factor / gain_half)[None]
    r_gc = remote(gcb.at[c], gcb.at[c], partner)

    recv(r_kz)
    ky_s[...] = (
        dot(perm_yz(), kz_r[...].reshape(slots, qcols)).astype(BF16).reshape(2 * NY, 2 * NZ, qcols)
    )
    r_ky = yc_exchange(ky_s, ky_r)
    ky_r[pl.ds(y * 2 + c, 1)] = ky_s[pl.ds(y * 2 + c, 1)]

    summed = []
    for yy in range(NY):
        ga[LA, yy].wait_recv()
        acc = gf[yy, pl.ds(z, 1)][0] + ra[LA - 1, yy].astype(F32)
        if LB:
            gb[LB, yy].wait_recv()
            acc = acc + rb[LB - 1, yy].astype(F32)
        gy_s[yy] = acc.astype(BF16)
    r_gyx = []
    for d in range(1, NY):
        yy = lax.rem(y + d, NY)
        r_gyx.append(remote(gy_s.at[yy], gy_r.at[y], at_dp(yy, z, c)))
    gy_r[pl.ds(y, 1)] = gy_s[pl.ds(y, 1)]

    recv(r_ky)
    kout[pl.ds(x, 1)] = (
        dot(perm_out(), ky_r[...].reshape(slots, qcols)).astype(BF16)[None]
    )
    r_ko = []
    for d in range(1, NX):
        r_ko.append(remote(kout.at[x], kout.at[x], {"tensor": h * NX + lax.rem(x + d, NX)}))

    recv(r_gyx)
    acc = gy_r[0].astype(F32)
    for i in range(1, NY):
        acc = acc + gy_r[i].astype(F32)
    acc = acc * factor
    low, high = acc[: acc.shape[0] // 2], acc[acc.shape[0] // 2 :]
    gc_s[...] = jnp.where(c == 0, high, low)
    r_gcx = remote(gc_s, gout.at[c], partner)
    gout[pl.ds(c, 1)] = jnp.where(c == 0, low, high)[None]

    r_gc.wait_recv()
    outs = [local(gcb.at[i], gg_out.at[:, i * half : (i + 1) * half]) for i in range(2)]
    r_gcx.wait_recv()
    outs += [local(gout.at[i], gw_out.at[:, i * half : (i + 1) * half]) for i in range(2)]
    recv(r_ko)
    outs += [
        local(kout.at[q], keys_out.at[0, :, q * qcols : (q + 1) * qcols]) for q in range(NX)
    ]
    for d in sends:
        d.wait_send()
    for d in outs:
        d.wait()


def build(mesh, dims):
    NY, NZ, NH, NX = dims
    LA, LB = NZ // 2, NZ // 2 - 1

    def on_device(hidden_rows, norm_gain, key_weight, cotangent, accepted_counts, destination):
        rows, cols = hidden_rows.shape
        half = cols // 2
        kvw = cotangent.shape[2]
        slots = 2 * rows
        kr = key_weight.shape[0]
        qcols = kvw // NX
        factor = 1.0 / math.sqrt(rows * lax.axis_size("dp"))
        V = pltpu.VMEM
        ncopies = 200
        scratch = [
            V((2, rows, half), BF16),
            V((kr, half), BF16),
            V((kr, half), BF16),
            V((NY, NZ, 2 * kr, half), BF16),
            V((slots, kvw), BF16),
            V((NZ, 4 * NY, kvw), BF16),
            V((NZ, 4 * NY, kvw), BF16),
            V((2 * NY, 2 * NZ, kvw), BF16),
            V((2 * NY, 2 * NZ, kvw), BF16),
            V((2, rows, kvw), BF16),
            V((NH * NX, 1, 2 * rows), F32),
            V((2, 1, 2 * rows), F32),
            V((2 * rows, half), BF16),
            V((NY, NZ, 2 * kr, half), F32),
            V((NY, NZ, 2 * kr, half), BF16),
            V((LA, NY, 2 * kr, half), BF16),
            V((max(LB, 1), NY, 2 * kr, half), BF16),
            V((max(LA - 1, 1), NY, 2 * kr, half), BF16),
            V((max(LB - 1, 1), NY, 2 * kr, half), BF16),
            V((NY, 2 * kr, half), BF16),
            V((NY, 2 * kr, half), BF16),
            V((kr, half), F32),
            V((2, kr, half), F32),
            V((NZ, 1, half), F32),
            V((NY, 1, half), F32),
            V((2, 1, half), F32),
            V((2 * rows, kvw), F32),
            V((rows, kvw), F32),
            V((rows, kvw), F32),
            V((NX, rows, qcols), BF16),
            V((NX, rows, qcols), BF16),
            V((rows, qcols), BF16),
            V((rows, qcols), BF16),
            V((NZ, 4 * NY, qcols), BF16),
            V((NZ, 4 * NY, qcols), BF16),
            V((2 * NY, 2 * NZ, qcols), BF16),
            V((2 * NY, 2 * NZ, qcols), BF16),
            V((NX, slots, qcols), BF16),
            pltpu.SemaphoreType.DMA((ncopies,)),
            pltpu.SemaphoreType.DMA((ncopies,)),
            pltpu.SemaphoreType.DMA((16,)),
        ]
        any_spec = pl.BlockSpec(memory_space=pl.ANY)
        vmem = pl.BlockSpec(memory_space=pltpu.VMEM)
        smem = pl.BlockSpec(memory_space=pltpu.SMEM)
        keys, gw, gg = pl.pallas_call(
            functools.partial(kernel, dims, factor),
            out_shape=(
                jax.ShapeDtypeStruct((1, slots, kvw), BF16),
                jax.ShapeDtypeStruct((kr, cols), F32),
                jax.ShapeDtypeStruct((1, cols), F32),
            ),
            in_specs=[any_spec, vmem, any_spec, any_spec, smem, vmem],
            out_specs=(any_spec, any_spec, any_spec),
            scratch_shapes=scratch,
            compiler_params=pltpu.CompilerParams(collective_id=0, has_side_effects=True),
        )(
            hidden_rows,
            norm_gain.reshape(1, cols),
            key_weight,
            cotangent,
            accepted_counts,
            destination.reshape(1, rows),
        )
        return keys, gw, gg.reshape(cols)

    return jax.shard_map(
        on_device,
        mesh=mesh,
        in_specs=(
            P("dp", "tensor"),
            P("tensor"),
            P("dp", "tensor"),
            P("dp", None, None),
            P("dp"),
            P("dp"),
        ),
        out_specs=(P("dp", None, None), P("dp", "tensor"), P("tensor")),
        check_vma=False,
    )


def solution(mesh):
    return build(mesh, (4, 8, 2, 4))
```

```python
import functools
import math

import jax
import jax.numpy as jnp
from jax import lax
from jax.experimental import pallas as pl
from jax.experimental.pallas import tpu as pltpu
from jax.sharding import PartitionSpec as P

EPSILON = 1e-05
F32 = jnp.float32
BF16 = jnp.bfloat16
MESH = pl.DeviceIdType.MESH


def iota(shape, dim):
    return lax.broadcasted_iota(jnp.int32, shape, dim)


def onehot(cond):
    return jnp.where(cond, 1.0, 0.0).astype(BF16)


def kernel(
    dims,
    factor,
    hid,
    gain_ref,
    wsh,
    cot,
    count_ref,
    dest_ref,
    keys_out,
    gw_out,
    gg_out,
    hown,
    hbuf,
    wall,
    permz,
    permo,
    pick,
    place,
    cotv,
    cot_a,
    cot_b1,
    cot_s,
    cot_b2,
    cot_r,
    sqb,
    sqc,
    norm,
    gf,
    gs,
    ra,
    rb,
    sa,
    sb,
    gy_s,
    gy_r,
    gc_s,
    gout,
    gz,
    gyb,
    gcb,
    k_part,
    kx_s,
    kx_r,
    kz_s,
    kz_r,
    ky_s,
    ky_r,
    kout,
    ssem,
    rsem,
    lsem,
):
    NY, NZ, NH, NX = dims
    NT = NH * NX
    dp = lax.axis_index("dp")
    t = lax.axis_index("tensor")
    c = lax.rem(dp, 2)
    z = lax.rem(lax.div(dp, 2), NZ)
    y = lax.div(dp, 2 * NZ)
    x = lax.rem(t, NX)
    h = lax.div(t, NX)
    rows = dest_ref.shape[1]
    slots = 2 * rows
    half = hbuf.shape[2]
    width = half * 2 * NT
    kvw = cotv.shape[1]
    qcols = kvw // NX
    sign = 1 - 2 * c
    LA, LB = NZ // 2, NZ // 2 - 1

    def at_dp(yy, zz, cc):
        return {"dp": (yy * NZ + zz) * 2 + cc}

    partner = at_dp(y, z, 1 - c)
    z_fwd = at_dp(y, lax.rem(z + sign + NZ, NZ), c)
    z_bwd = at_dp(y, lax.rem(z - sign + NZ, NZ), c)

    def zmod(v):
        return lax.rem(v + 2 * NZ, NZ)

    counter = [0]
    sends = []

    def remote(src, dst, dev):
        i = counter[0]
        counter[0] += 1
        d = pltpu.make_async_remote_copy(
            src_ref=src,
            dst_ref=dst,
            send_sem=ssem.at[i],
            recv_sem=rsem.at[i],
            device_id=dev,
            device_id_type=MESH,
        )
        d.start()
        sends.append(d)
        return d

    lcount = [0]

    def local(src, dst):
        i = lcount[0]
        lcount[0] += 1
        d = pltpu.make_async_copy(src, dst, lsem.at[i])
        d.start()
        return d

    own_cols = pl.ds(pl.multiple_of(c * half, half), half)
    other_cols = pl.ds(pl.multiple_of((1 - c) * half, half), half)

    barrier = pltpu.get_barrier_semaphore()
    peers = []
    for d in range(1, NZ):
        peers.append(at_dp(y, lax.rem(z + d, NZ), c))
    for dy in range(NY):
        for dc in range(2):
            if dy or dc:
                peers.append(at_dp(lax.rem(y + dy, NY), z, lax.rem(c + dc, 2)))
    for d in range(1, NT):
        peers.append({"tensor": lax.rem(t + d, NT)})
    for d in range(1, NX):
        peers.append(dict(at_dp(y, z, 1 - c), tensor=h * NX + lax.rem(x + d, NX)))
    for dy in range(NY):
        for dc in range(2):
            for dh in range(1, NH):
                if dy or dc:
                    peers.append(
                        dict(
                            at_dp(lax.rem(y + dy, NY), z, lax.rem(c + dc, 2)),
                            tensor=lax.rem(h + dh, NH) * NX + x,
                        )
                    )
    for p in peers:
        pl.semaphore_signal(barrier, inc=1, device_id=p, device_id_type=MESH)

    l_cot = local(cot.at[0], cotv)
    l_own = local(hid, hown)
    l_w = local(wsh.at[:, own_cols], wall.at[y, z, c])
    l_h = local(hid.at[:, own_cols], hbuf.at[c])

    def perm_zy():
        b = iota((slots, slots), 1)
        bz = (b // 4) % NZ
        by = b // (4 * NZ)
        return onehot(iota((slots, slots), 0) == bz * (4 * NY) + by * 4 + b % 4)

    def perm_yz():
        b = iota((slots, slots), 1)
        bz = b // (4 * NY)
        byc = (b // 2) % (2 * NY)
        return onehot(iota((slots, slots), 0) == byc * (2 * NZ) + bz * 2 + b % 2)

    def perm_out():
        b = iota((slots, slots), 1)
        by = b // (4 * NZ)
        bc = (b // (2 * NZ)) % 2
        bz = (b // 2) % NZ
        return onehot(iota((slots, slots), 0) == by * (4 * NZ) + bz * 4 + bc * 2 + b % 2)

    def dot(a, b):
        return jnp.dot(a, b, preferred_element_type=F32)

    l_cot.wait()
    mixed = dot(perm_zy(), cotv[...]).astype(BF16)
    cot_a[...] = mixed.reshape(NZ, 4 * NY, kvw)

    l_own.wait()
    eye = iota((rows, rows), 0) == iota((rows, rows), 1)

    def as_row(col):
        return jnp.sum(jnp.where(eye, col, 0.0), axis=0, keepdims=True)

    def as_col(row):
        return jnp.sum(jnp.where(eye, row, 0.0), axis=1, keepdims=True)

    values = hown[...].astype(F32)
    sqb[pl.ds(t, 1)] = as_row(jnp.sum(values * values, axis=1, keepdims=True))[None]

    permz[...] = perm_yz()
    permo[...] = perm_out()
    drow = dest_ref[...]
    dcol = as_col(drow.astype(F32)).astype(jnp.int32)
    same = dcol == drow
    rank_col = jnp.sum(
        jnp.where(same & (iota((rows, rows), 1) < iota((rows, rows), 0)), 1.0, 0.0),
        axis=1,
        keepdims=True,
    ).astype(jnp.int32)
    rank_row = jnp.sum(
        jnp.where(same & (iota((rows, rows), 0) < iota((rows, rows), 1)), 1.0, 0.0),
        axis=0,
        keepdims=True,
    ).astype(jnp.int32)
    count = count_ref[...]

    def yc_of(dest):
        return (dest // (2 * NZ)) * 2 + dest % 2

    def z_of(dest):
        return (dest // 2) % NZ

    pos_col = yc_of(dcol) * (2 * NZ) + z_of(dcol) * 2 + rank_col
    pick[...] = onehot((iota((rows, slots), 1) == pos_col) & (iota((rows, slots), 0) < count))
    pos_row = z_of(drow) * (4 * NY) + yc_of(drow) * 2 + rank_row
    place[...] = onehot((iota((slots, rows), 0) == pos_row) & (iota((slots, rows), 1) < count))

    pl.semaphore_wait(barrier, len(peers))

    r_wy = {}
    for d in range(NY):
        for dc in range(2):
            if d or dc:
                cc = lax.rem(c + dc, 2)
                r_wy[d, dc] = remote(
                    wsh.at[:, other_cols if dc else own_cols],
                    wall.at[y, z, c],
                    at_dp(lax.rem(y + d, NY), z, cc),
                )

    def z_exchange(src, dst):
        return [
            remote(src.at[lax.rem(z + d, NZ)], dst.at[z], at_dp(y, lax.rem(z + d, NZ), c))
            for d in range(1, NZ)
        ]

    def yc_exchange(src, dst):
        out = []
        for dy in range(NY):
            for dc in range(2):
                if dy or dc:
                    yy, cc = lax.rem(y + dy, NY), lax.rem(c + dc, 2)
                    out.append(remote(src.at[yy * 2 + cc], dst.at[y * 2 + c], at_dp(yy, z, cc)))
        return out

    def recv(copies):
        for d in copies:
            d.wait_recv()

    r_cz = z_exchange(cot_a, cot_b1)
    cot_b1[pl.ds(z, 1)] = cot_a[pl.ds(z, 1)]
    r_sq = [
        remote(sqb.at[t], sqb.at[t], {"tensor": lax.rem(t + d, NT)}) for d in range(1, NT)
    ]
    r_h = remote(hid.at[:, other_cols], hbuf.at[c], partner)

    def w_send(step, d, fwd):
        yy = lax.rem(y - d + NY, NY)
        zz = zmod(z - (step - 1) * sign) if fwd else zmod(z + (step - 1) * sign)
        return remote(wall.at[yy, zz], wall.at[yy, zz], z_fwd if fwd else z_bwd)

    wa, wb = {}, {}

    def w_step(step, d):
        if step <= LA:
            wa[step, d] = w_send(step, d, True)
        if step <= LB:
            wb[step, d] = w_send(step, d, False)

    def w_recv(step, d):
        if step <= LA:
            wa[step, d].wait_recv()
        if step <= LB:
            wb[step, d].wait_recv()

    l_w.wait()
    r_wy[0, 1].wait_recv()
    w_step(1, 0)
    for d in range(1, NY):
        r_wy[d, 0].wait_recv()
        r_wy[d, 1].wait_recv()
        w_step(1, d)

    w_recv(1, 0)
    w_step(2, 0)

    recv(r_cz)
    cot_s[...] = (
        dot(permz[...], cot_b1[...].reshape(slots, kvw)).astype(BF16).reshape(2 * NY, 2 * NZ, kvw)
    )
    r_cy = yc_exchange(cot_s, cot_b2)
    cot_b2[pl.ds(y * 2 + c, 1)] = cot_s[pl.ds(y * 2 + c, 1)]

    for d in range(1, NY):
        w_recv(1, d)
        w_step(2, d)

    recv(r_sq)
    total = sqb[0]
    for i in range(1, NT):
        total = total + sqb[i]
    sqc[pl.ds(c, 1)] = total[None]
    r_sc = remote(sqc.at[c], sqc.at[c], partner)

    for d in range(NY):
        w_recv(2, d)
        w_step(3, d)

    recv(r_cy)
    cot_r[pl.ds(c, 1)] = dot(pick[...], cot_b2[...].reshape(slots, kvw)).astype(BF16)[None]
    r_cr = remote(cot_r.at[c], cot_r.at[c], partner)

    for step in range(3, LA):
        for d in range(NY):
            w_recv(step, d)
            w_step(step + 1, d)

    l_h.wait()
    r_h.wait_recv()
    r_sc.wait_recv()
    gain_half = gain_ref[:, own_cols]
    for i in range(2):
        scale = as_col(lax.rsqrt(sqc[i] / width + EPSILON))
        norm[i * rows : (i + 1) * rows] = (hbuf[i].astype(F32) * scale * gain_half).astype(BF16)

    r_cr.wait_recv()
    cot2 = cot_r[...].reshape(2 * rows, kvw)
    kb = kvw // NY
    for yy in range(NY):
        part = lax.dot_general(
            cot2[:, yy * kb : (yy + 1) * kb],
            norm[...],
            (((0,), (0,)), ((), ())),
            preferred_element_type=F32,
        ).reshape(NZ, kb // NZ, half)
        gf[yy] = part
        gs[yy] = part.astype(BF16)

    ga, gb = {}, {}
    order = list(range(1, NY)) + [0]
    za1, zb1 = zmod(z + LA * sign), zmod(z - LB * sign)

    def y_of(j):
        return lax.rem(y + j, NY)

    def own_g(j, zz):
        return gf[pl.ds(y_of(j), 1), pl.ds(zz, 1)][0, 0]

    for j in order:
        ga[1, j] = remote(gs.at[y_of(j), za1], ra.at[0, j], z_fwd)
        if LB:
            gb[1, j] = remote(gs.at[y_of(j), zb1], rb.at[0, j], z_bwd)

    def g_step(step):
        for j in order:
            if step <= LA:
                ga[step - 1, j].wait_recv()
                own = own_g(j, zmod(z + (LA + 1 - step) * sign))
                sa[step - 2, j] = (ra[step - 2, j].astype(F32) + own).astype(BF16)
                ga[step, j] = remote(sa.at[step - 2, j], ra.at[step - 1, j], z_fwd)
            if step <= LB:
                gb[step - 1, j].wait_recv()
                own = own_g(j, zmod(z - (LB + 1 - step) * sign))
                sb[step - 2, j] = (rb[step - 2, j].astype(F32) + own).astype(BF16)
                gb[step, j] = remote(sb.at[step - 2, j], rb.at[step - 1, j], z_bwd)

    if LA > 2:
        for d in range(NY):
            w_recv(LA, d)

    for yy in range(NY):
        k_part[:, yy * kb : (yy + 1) * kb] = lax.dot_general(
            norm[...],
            wall[yy].reshape(kb, half),
            (((1,), (1,)), ((), ())),
            preferred_element_type=F32,
        )
    for q in range(NX):
        block = k_part[:, q * qcols : (q + 1) * qcols].astype(BF16)
        kx_s[q] = block.reshape(2, rows, qcols)
    r_kx = []
    for dc in range(2):
        for d in range(NX):
            if d or dc:
                xx, cc = lax.rem(x + d, NX), lax.rem(c + dc, 2)
                r_kx.append(
                    remote(
                        kx_s.at[xx, cc],
                        kx_r.at[x, c],
                        dict(at_dp(y, z, cc), tensor=h * NX + xx),
                    )
                )
    kx_r[pl.ds(x, 1), pl.ds(c, 1)] = kx_s[pl.ds(x, 1), pl.ds(c, 1)]

    gain_sum = jnp.zeros((1, half), F32)
    for yy in range(NY):
        gain_sum += jnp.sum(
            gf[yy].reshape(kb, half) * wall[yy].reshape(kb, half).astype(F32), axis=0, keepdims=True
        )
    gz[pl.ds(z, 1)] = gain_sum[None]
    r_gz = [
        remote(gz.at[z], gz.at[z], at_dp(y, lax.rem(z + d, NZ), c)) for d in range(1, NZ)
    ]

    if LA >= 2:
        g_step(2)

    recv(r_kx)
    mine_k = kx_r[0, 0].astype(F32)
    for i in range(1, 2 * NX):
        mine_k = mine_k + kx_r[i // 2, i % 2].astype(F32)
    kz_s[...] = dot(place[...], mine_k.astype(BF16)).astype(BF16).reshape(NZ, 4 * NY, qcols)
    r_kz = z_exchange(kz_s, kz_r)
    kz_r[pl.ds(z, 1)] = kz_s[pl.ds(z, 1)]

    recv(r_gz)
    gain_sum = gz[0]
    for i in range(1, NZ):
        gain_sum = gain_sum + gz[i]
    gyb[pl.ds(y, 1)] = gain_sum[None]
    r_gy = [
        remote(gyb.at[y], gyb.at[y], at_dp(lax.rem(y + d, NY), z, c)) for d in range(1, NY)
    ]

    if LA >= 3:
        g_step(3)

    for step in range(4, LA + 1):
        g_step(step)

    recv(r_gy)
    gain_sum = gyb[0]
    for i in range(1, NY):
        gain_sum = gain_sum + gyb[i]
    gcb[pl.ds(c, 1)] = (gain_sum * factor / gain_half)[None]
    r_gc = remote(gcb.at[c], gcb.at[c], partner)

    recv(r_kz)
    ky_s[...] = (
        dot(permz[...], kz_r[...].reshape(slots, qcols)).astype(BF16).reshape(2 * NY, 2 * NZ, qcols)
    )
    r_ky = []
    for dh in range(NH):
        for dy in range(NY):
            for dc in range(2):
                if dy or dc or dh:
                    yy, cc, hh = lax.rem(y + dy, NY), lax.rem(c + dc, 2), lax.rem(h + dh, NH)
                    r_ky.append(
                        remote(
                            ky_s.at[yy * 2 + cc],
                            ky_r.at[h, y * 2 + c],
                            dict(at_dp(yy, z, cc), tensor=hh * NX + x),
                        )
                    )
    ky_r[pl.ds(h, 1), pl.ds(y * 2 + c, 1)] = ky_s[pl.ds(y * 2 + c, 1)][None]

    r_gyx = []
    for j in order:
        ga[LA, j].wait_recv()
        acc = own_g(j, z) + ra[LA - 1, j].astype(F32)
        if LB:
            gb[LB, j].wait_recv()
            acc = acc + rb[LB - 1, j].astype(F32)
        if j:
            gy_s[j] = acc.astype(BF16)
            r_gyx.append(remote(gy_s.at[j], gy_r.at[j], at_dp(y_of(j), z, c)))

    recv(r_ky)
    whole = ky_r[0].astype(F32)
    for i in range(1, NH):
        whole = whole + ky_r[i].astype(F32)
    kout[pl.ds(x, 1)] = (
        dot(permo[...], whole.astype(BF16).reshape(slots, qcols)).astype(BF16)[None]
    )
    r_ko = []
    for d in range(1, NX):
        r_ko.append(remote(kout.at[x], kout.at[x], {"tensor": h * NX + lax.rem(x + d, NX)}))

    recv(r_gyx)
    for i in range(1, NY):
        acc = acc + gy_r[i].astype(F32)
    acc = acc * factor
    low, high = acc[: acc.shape[0] // 2], acc[acc.shape[0] // 2 :]
    gc_s[...] = jnp.where(c == 0, high, low)
    r_gcx = remote(gc_s, gout.at[c], partner)
    gout[pl.ds(c, 1)] = jnp.where(c == 0, low, high)[None]

    r_gc.wait_recv()
    outs = [local(gcb.at[i], gg_out.at[:, i * half : (i + 1) * half]) for i in range(2)]
    r_gcx.wait_recv()
    outs += [local(gout.at[i], gw_out.at[:, i * half : (i + 1) * half]) for i in range(2)]
    recv(r_ko)
    outs += [
        local(kout.at[q], keys_out.at[0, :, q * qcols : (q + 1) * qcols]) for q in range(NX)
    ]
    for d in sends:
        d.wait_send()
    for d in outs:
        d.wait()


def write_out(k_in, gw_in, gg_in, k_out, gw_out, gg_out, sem):
    pairs = ((k_in, k_out), (gw_in, gw_out), (gg_in, gg_out))
    copies = [pltpu.make_async_copy(a, b, sem.at[i]) for i, (a, b) in enumerate(pairs)]
    for d in copies:
        d.start()
    for d in copies:
        d.wait()


def build(mesh, dims):
    NY, NZ, NH, NX = dims
    LA, LB = NZ // 2, NZ // 2 - 1

    def on_device(hidden_rows, norm_gain, key_weight, cotangent, accepted_counts, destination):
        rows, cols = hidden_rows.shape
        half = cols // 2
        kvw = cotangent.shape[2]
        slots = 2 * rows
        kr = key_weight.shape[0]
        qcols = kvw // NX
        factor = 1.0 / math.sqrt(rows * lax.axis_size("dp"))
        V = pltpu.VMEM
        ncopies = 200
        scratch = [
            V((rows, cols), BF16),
            V((2, rows, half), BF16),
            V((NY, NZ, 2, kr, half), BF16),
            V((slots, slots), BF16),
            V((slots, slots), BF16),
            V((rows, slots), BF16),
            V((slots, rows), BF16),
            V((slots, kvw), BF16),
            V((NZ, 4 * NY, kvw), BF16),
            V((NZ, 4 * NY, kvw), BF16),
            V((2 * NY, 2 * NZ, kvw), BF16),
            V((2 * NY, 2 * NZ, kvw), BF16),
            V((2, rows, kvw), BF16),
            V((NH * NX, 1, rows), F32),
            V((2, 1, rows), F32),
            V((2 * rows, half), BF16),
            V((NY, NZ, 2 * kr, half), F32),
            V((NY, NZ, 2 * kr, half), BF16),
            V((LA, NY, 2 * kr, half), BF16),
            V((max(LB, 1), NY, 2 * kr, half), BF16),
            V((max(LA - 1, 1), NY, 2 * kr, half), BF16),
            V((max(LB - 1, 1), NY, 2 * kr, half), BF16),
            V((NY, 2 * kr, half), BF16),
            V((NY, 2 * kr, half), BF16),
            V((kr, half), F32),
            V((2, kr, half), F32),
            V((NZ, 1, half), F32),
            V((NY, 1, half), F32),
            V((2, 1, half), F32),
            V((2 * rows, kvw), F32),
            V((NX, 2, rows, qcols), BF16),
            V((NX, 2, rows, qcols), BF16),
            V((NZ, 4 * NY, qcols), BF16),
            V((NZ, 4 * NY, qcols), BF16),
            V((2 * NY, 2 * NZ, qcols), BF16),
            V((NH, 2 * NY, 2 * NZ, qcols), BF16),
            V((NX, slots, qcols), BF16),
            pltpu.SemaphoreType.DMA((ncopies,)),
            pltpu.SemaphoreType.DMA((ncopies,)),
            pltpu.SemaphoreType.DMA((16,)),
        ]
        any_spec = pl.BlockSpec(memory_space=pl.ANY)
        vmem = pl.BlockSpec(memory_space=pltpu.VMEM)
        keys, gw, gg = pl.pallas_call(
            functools.partial(kernel, dims, factor),
            out_shape=(
                jax.ShapeDtypeStruct((1, slots, kvw), BF16),
                jax.ShapeDtypeStruct((kr, cols), F32),
                jax.ShapeDtypeStruct((1, cols), F32),
            ),
            in_specs=[any_spec, vmem, any_spec, any_spec, vmem, vmem],
            out_specs=(vmem, vmem, vmem),
            scratch_shapes=scratch,
            compiler_params=pltpu.CompilerParams(collective_id=0, has_side_effects=True),
            name="exchange",
        )(
            hidden_rows,
            norm_gain.reshape(1, cols),
            key_weight,
            cotangent,
            accepted_counts.reshape(1, 1),
            destination.reshape(1, rows),
        )
        keys, gw, gg = pl.pallas_call(
            write_out,
            out_shape=tuple(jax.ShapeDtypeStruct(a.shape, a.dtype) for a in (keys, gw, gg)),
            in_specs=[vmem] * 3,
            out_specs=(any_spec,) * 3,
            scratch_shapes=[pltpu.SemaphoreType.DMA((3,))],
            name="results",
        )(keys, gw, gg)
        return keys, gw, gg.reshape(cols)

    return jax.shard_map(
        on_device,
        mesh=mesh,
        in_specs=(
            P("dp", "tensor"),
            P("tensor"),
            P("dp", "tensor"),
            P("dp", None, None),
            P("dp"),
            P("dp"),
        ),
        out_specs=(P("dp", None, None), P("dp", "tensor"), P("tensor")),
        check_vma=False,
    )


def solution(mesh):
    return build(mesh, (4, 8, 2, 4))
```

```python
import functools
import math

import jax
import jax.numpy as jnp
from jax import lax
from jax.experimental import pallas as pl
from jax.experimental.pallas import tpu as pltpu
from jax.sharding import PartitionSpec as P

EPSILON = 1e-05
F32 = jnp.float32
BF16 = jnp.bfloat16
MESH = pl.DeviceIdType.MESH


def iota(shape, dim):
    return lax.broadcasted_iota(jnp.int32, shape, dim)


def onehot(cond):
    return jnp.where(cond, 1.0, 0.0).astype(BF16)


def kernel(
    dims,
    factor,
    hid,
    gain_ref,
    wsh,
    cot,
    count_ref,
    dest_ref,
    keys_out,
    gw_out,
    gg_out,
    hown,
    wown,
    hbuf,
    wall,
    permz,
    permo,
    pick,
    place,
    cotv,
    cot_a,
    cot_b1,
    cot_s,
    cot_b2,
    cot_r,
    sqb,
    sqc,
    norm,
    gf,
    gs,
    rj,
    ra,
    rb,
    sa,
    sb,
    gy_s,
    gy_r,
    gc_s,
    gout,
    gz,
    gyb,
    gcb,
    kx_s,
    kx_r,
    kz_s,
    kz_r,
    ky_s,
    ky_r,
    kout,
    ssem,
    rsem,
    lsem,
):
    NY, NZ, NH, NX = dims
    NT = NH * NX
    dp = lax.axis_index("dp")
    t = lax.axis_index("tensor")
    c = lax.rem(dp, 2)
    z = lax.rem(lax.div(dp, 2), NZ)
    y = lax.div(dp, 2 * NZ)
    x = lax.rem(t, NX)
    h = lax.div(t, NX)
    rows = dest_ref.shape[1]
    slots = 2 * rows
    half = hbuf.shape[2]
    width = half * 2 * NT
    kvw = cotv.shape[1]
    qcols = kvw // NX
    sign = 1 - 2 * c
    LA, LB = NZ // 2, NZ // 2 - 1

    def at_dp(yy, zz, cc):
        return {"dp": (yy * NZ + zz) * 2 + cc}

    partner = at_dp(y, z, 1 - c)
    z_fwd = at_dp(y, lax.rem(z + sign + NZ, NZ), c)
    z_bwd = at_dp(y, lax.rem(z - sign + NZ, NZ), c)
    z_jump = at_dp(y, lax.rem(z + 2 * sign + NZ, NZ), c)

    def zmod(v):
        return lax.rem(v + 2 * NZ, NZ)

    counter = [0]
    sends = []

    def remote(src, dst, dev):
        i = counter[0]
        counter[0] += 1
        d = pltpu.make_async_remote_copy(
            src_ref=src,
            dst_ref=dst,
            send_sem=ssem.at[i],
            recv_sem=rsem.at[i],
            device_id=dev,
            device_id_type=MESH,
        )
        d.start()
        sends.append(d)
        return d

    lcount = [0]

    def local(src, dst):
        i = lcount[0]
        lcount[0] += 1
        d = pltpu.make_async_copy(src, dst, lsem.at[i])
        d.start()
        return d

    own_cols = pl.ds(pl.multiple_of(c * half, half), half)
    other_cols = pl.ds(pl.multiple_of((1 - c) * half, half), half)

    barrier = pltpu.get_barrier_semaphore()
    peers = []
    for d in range(1, NZ):
        peers.append(at_dp(y, lax.rem(z + d, NZ), c))
    for dy in range(NY):
        for dc in range(2):
            if dy or dc:
                peers.append(at_dp(lax.rem(y + dy, NY), z, lax.rem(c + dc, 2)))
    for d in range(1, NT):
        peers.append({"tensor": lax.rem(t + d, NT)})
    for d in range(1, NX):
        peers.append(dict(at_dp(y, z, 1 - c), tensor=h * NX + lax.rem(x + d, NX)))
    for dy in range(NY):
        for dc in range(2):
            for dh in range(1, NH):
                if dy or dc:
                    peers.append(
                        dict(
                            at_dp(lax.rem(y + dy, NY), z, lax.rem(c + dc, 2)),
                            tensor=lax.rem(h + dh, NH) * NX + x,
                        )
                    )
    for p in peers:
        pl.semaphore_signal(barrier, inc=1, device_id=p, device_id_type=MESH)

    l_cot = local(cot.at[0], cotv)
    l_own = local(hid, hown)
    l_wv = local(wsh, wown)
    l_w = local(wsh.at[:, own_cols], wall.at[y, z, c])
    l_h = local(hid.at[:, own_cols], hbuf.at[c])

    def perm_zy():
        b = iota((slots, slots), 1)
        bz = (b // 4) % NZ
        by = b // (4 * NZ)
        return onehot(iota((slots, slots), 0) == bz * (4 * NY) + by * 4 + b % 4)

    def perm_yz():
        b = iota((slots, slots), 1)
        bz = b // (4 * NY)
        byc = (b // 2) % (2 * NY)
        return onehot(iota((slots, slots), 0) == byc * (2 * NZ) + bz * 2 + b % 2)

    def perm_out():
        b = iota((slots, slots), 1)
        by = b // (4 * NZ)
        bc = (b // (2 * NZ)) % 2
        bz = (b // 2) % NZ
        return onehot(iota((slots, slots), 0) == by * (4 * NZ) + bz * 4 + bc * 2 + b % 2)

    def dot(a, b):
        return jnp.dot(a, b, preferred_element_type=F32)

    l_cot.wait()
    mixed = dot(perm_zy(), cotv[...]).astype(BF16)
    cot_a[...] = mixed.reshape(NZ, 4 * NY, kvw)

    l_own.wait()
    eye = iota((rows, rows), 0) == iota((rows, rows), 1)

    def as_row(col):
        return jnp.sum(jnp.where(eye, col, 0.0), axis=0, keepdims=True)

    def as_col(row):
        return jnp.sum(jnp.where(eye, row, 0.0), axis=1, keepdims=True)

    values = hown[...].astype(F32)
    sqb[pl.ds(t, 1)] = as_row(jnp.sum(values * values, axis=1, keepdims=True))[None]

    permz[...] = perm_yz()
    permo[...] = perm_out()
    drow = dest_ref[...]
    dcol = as_col(drow.astype(F32)).astype(jnp.int32)
    same = dcol == drow
    rank_col = jnp.sum(
        jnp.where(same & (iota((rows, rows), 1) < iota((rows, rows), 0)), 1.0, 0.0),
        axis=1,
        keepdims=True,
    ).astype(jnp.int32)
    rank_row = jnp.sum(
        jnp.where(same & (iota((rows, rows), 0) < iota((rows, rows), 1)), 1.0, 0.0),
        axis=0,
        keepdims=True,
    ).astype(jnp.int32)
    count = count_ref[...]

    def yc_of(dest):
        return (dest // (2 * NZ)) * 2 + dest % 2

    def z_of(dest):
        return (dest // 2) % NZ

    pos_col = yc_of(dcol) * (2 * NZ) + z_of(dcol) * 2 + rank_col
    pick[...] = onehot((iota((rows, slots), 1) == pos_col) & (iota((rows, slots), 0) < count))
    pos_row = z_of(drow) * (4 * NY) + yc_of(drow) * 2 + rank_row
    place[...] = onehot((iota((slots, rows), 0) == pos_row) & (iota((slots, rows), 1) < count))

    l_wv.wait()
    pl.semaphore_wait(barrier, len(peers))

    r_wy = {}
    for d in range(NY):
        for dc in range(2):
            if d or dc:
                cc = lax.rem(c + dc, 2)
                r_wy[d, dc] = remote(
                    wown.at[:, other_cols if dc else own_cols],
                    wall.at[y, z, c],
                    at_dp(lax.rem(y + d, NY), z, cc),
                )

    def z_exchange(src, dst):
        return [
            remote(src.at[lax.rem(z + d, NZ)], dst.at[z], at_dp(y, lax.rem(z + d, NZ), c))
            for d in range(1, NZ)
        ]

    def yc_exchange(src, dst):
        out = []
        for dy in range(NY):
            for dc in range(2):
                if dy or dc:
                    yy, cc = lax.rem(y + dy, NY), lax.rem(c + dc, 2)
                    out.append(remote(src.at[yy * 2 + cc], dst.at[y * 2 + c], at_dp(yy, z, cc)))
        return out

    def recv(copies):
        for d in copies:
            d.wait_recv()

    r_cz = z_exchange(cot_a, cot_b1)
    cot_b1[pl.ds(z, 1)] = cot_a[pl.ds(z, 1)]
    r_sq = [
        remote(sqb.at[t], sqb.at[t], {"tensor": lax.rem(t + d, NT)}) for d in range(1, NT)
    ]
    r_h = remote(hown.at[:, other_cols], hbuf.at[c], partner)

    def w_send(step, d, fwd, to):
        yy = lax.rem(y - d + NY, NY)
        zz = zmod(z - (step - 1) * sign) if fwd else zmod(z + (step - 1) * sign)
        return remote(wall.at[yy, zz], wall.at[yy, zz], to)

    w_got = {}

    def w_step(step, d):
        if step <= LB:
            w_got[step, d] = [w_send(step, d, True, z_fwd), w_send(step, d, False, z_bwd)]
        if step == LB:
            w_got[LA, d] = [w_send(step, d, True, z_jump)]

    def w_recv(step, d):
        for r in w_got.pop((step, d), ()):
            r.wait_recv()

    l_w.wait()
    r_wy[0, 1].wait_recv()
    w_step(1, 0)
    for d in range(1, NY):
        r_wy[d, 0].wait_recv()
        r_wy[d, 1].wait_recv()
        w_step(1, d)

    w_recv(1, 0)
    w_step(2, 0)

    recv(r_cz)
    cot_s[...] = (
        dot(permz[...], cot_b1[...].reshape(slots, kvw)).astype(BF16).reshape(2 * NY, 2 * NZ, kvw)
    )
    r_cy = yc_exchange(cot_s, cot_b2)
    cot_b2[pl.ds(y * 2 + c, 1)] = cot_s[pl.ds(y * 2 + c, 1)]

    for d in range(1, NY):
        w_recv(1, d)
        w_step(2, d)

    recv(r_sq)
    total = sqb[0]
    for i in range(1, NT):
        total = total + sqb[i]
    sqc[pl.ds(c, 1)] = total[None]
    r_sc = remote(sqc.at[c], sqc.at[c], partner)

    for d in range(NY):
        w_recv(2, d)
        w_step(3, d)

    recv(r_cy)
    cot_r[pl.ds(c, 1)] = dot(pick[...], cot_b2[...].reshape(slots, kvw)).astype(BF16)[None]
    r_cr = remote(cot_r.at[c], cot_r.at[c], partner)

    l_h.wait()
    r_h.wait_recv()
    r_sc.wait_recv()
    gain_half = gain_ref[:, own_cols]
    for i in range(2):
        scale = as_col(lax.rsqrt(sqc[i] / width + EPSILON))
        norm[i * rows : (i + 1) * rows] = (hbuf[i].astype(F32) * scale * gain_half).astype(BF16)

    r_cr.wait_recv()
    cot2 = cot_r[...].reshape(2 * rows, kvw)
    kb = kvw // NY
    for yy in range(NY):
        part = lax.dot_general(
            cot2[:, yy * kb : (yy + 1) * kb],
            norm[...],
            (((0,), (0,)), ((), ())),
            preferred_element_type=F32,
        ).reshape(NZ, kb // NZ, half)
        gf[yy] = part
        gs[yy] = part.astype(BF16)

    ga, gb, gj = {}, {}, {}
    order = list(range(1, NY)) + [0]

    def y_of(j):
        return lax.rem(y + j, NY)

    def own_g(j, zz):
        return gf[pl.ds(y_of(j), 1), pl.ds(zz, 1)][0, 0]

    for j in order:
        ga[1, j] = remote(gs.at[y_of(j), zmod(z + LB * sign)], ra.at[0, j], z_fwd)
        gb[1, j] = remote(gs.at[y_of(j), zmod(z - LB * sign)], rb.at[0, j], z_bwd)
        gj[j] = remote(gs.at[y_of(j), zmod(z + LA * sign)], rj.at[j], z_jump)

    def g_step(step):
        if step > LB:
            return
        for j in order:
            ga[step - 1, j].wait_recv()
            acc = ra[step - 2, j].astype(F32) + own_g(j, zmod(z + (LA - step) * sign))
            if step == 2:
                gj[j].wait_recv()
                acc = acc + rj[j].astype(F32)
            sa[step - 2, j] = acc.astype(BF16)
            ga[step, j] = remote(sa.at[step - 2, j], ra.at[step - 1, j], z_fwd)
            gb[step - 1, j].wait_recv()
            acc = rb[step - 2, j].astype(F32) + own_g(j, zmod(z - (LA - step) * sign))
            sb[step - 2, j] = acc.astype(BF16)
            gb[step, j] = remote(sb.at[step - 2, j], rb.at[step - 1, j], z_bwd)

    for d in range(NY):
        for step in range(3, LA + 1):
            w_recv(step, d)
        yy = lax.rem(y - d + NY, NY)
        block = lax.dot_general(
            norm[...],
            wall[pl.ds(yy, 1)].reshape(kb, half),
            (((1,), (1,)), ((), ())),
            preferred_element_type=F32,
        )
        kx_s[pl.ds(yy, 1)] = block.astype(BF16).reshape(1, 2, rows, qcols)
    r_kx = []
    for dc in range(2):
        for d in range(NX):
            if d or dc:
                xx, cc = lax.rem(x + d, NX), lax.rem(c + dc, 2)
                r_kx.append(
                    remote(
                        kx_s.at[xx, cc],
                        kx_r.at[x, c],
                        dict(at_dp(y, z, cc), tensor=h * NX + xx),
                    )
                )
    kx_r[pl.ds(x, 1), pl.ds(c, 1)] = kx_s[pl.ds(x, 1), pl.ds(c, 1)]

    gain_sum = jnp.zeros((1, half), F32)
    for yy in range(NY):
        gain_sum += jnp.sum(
            gf[yy].reshape(kb, half) * wall[yy].reshape(kb, half).astype(F32), axis=0, keepdims=True
        )
    gz[pl.ds(z, 1)] = gain_sum[None]
    r_gz = [
        remote(gz.at[z], gz.at[z], at_dp(y, lax.rem(z + d, NZ), c)) for d in range(1, NZ)
    ]

    recv(r_kx)
    mine_k = kx_r[0, 0].astype(F32)
    for i in range(1, 2 * NX):
        mine_k = mine_k + kx_r[i // 2, i % 2].astype(F32)
    kz_s[...] = dot(place[...], mine_k.astype(BF16)).astype(BF16).reshape(NZ, 4 * NY, qcols)
    r_kz = z_exchange(kz_s, kz_r)
    kz_r[pl.ds(z, 1)] = kz_s[pl.ds(z, 1)]

    g_step(2)

    recv(r_gz)
    gain_sum = gz[0]
    for i in range(1, NZ):
        gain_sum = gain_sum + gz[i]
    gyb[pl.ds(y, 1)] = gain_sum[None]
    r_gy = [
        remote(gyb.at[y], gyb.at[y], at_dp(lax.rem(y + d, NY), z, c)) for d in range(1, NY)
    ]

    recv(r_kz)
    ky_s[...] = (
        dot(permz[...], kz_r[...].reshape(slots, qcols)).astype(BF16).reshape(2 * NY, 2 * NZ, qcols)
    )
    r_ky = []
    for dh in range(NH):
        for dy in range(NY):
            for dc in range(2):
                if dy or dc or dh:
                    yy, cc, hh = lax.rem(y + dy, NY), lax.rem(c + dc, 2), lax.rem(h + dh, NH)
                    r_ky.append(
                        remote(
                            ky_s.at[yy * 2 + cc],
                            ky_r.at[h, y * 2 + c],
                            dict(at_dp(yy, z, cc), tensor=hh * NX + x),
                        )
                    )
    ky_r[pl.ds(h, 1), pl.ds(y * 2 + c, 1)] = ky_s[pl.ds(y * 2 + c, 1)][None]

    g_step(3)

    recv(r_gy)
    gain_sum = gyb[0]
    for i in range(1, NY):
        gain_sum = gain_sum + gyb[i]
    gcb[pl.ds(c, 1)] = (gain_sum * factor / gain_half)[None]
    r_gc = remote(gcb.at[c], gcb.at[c], partner)

    r_gyx = []
    for j in order:
        ga[LB, j].wait_recv()
        gb[LB, j].wait_recv()
        acc = own_g(j, z) + ra[LB - 1, j].astype(F32) + rb[LB - 1, j].astype(F32)
        if LB == 1:
            gj[j].wait_recv()
            acc = acc + rj[j].astype(F32)
        if j:
            gy_s[j] = acc.astype(BF16)
            r_gyx.append(remote(gy_s.at[j], gy_r.at[j], at_dp(y_of(j), z, c)))

    recv(r_ky)
    whole = ky_r[0].astype(F32)
    for i in range(1, NH):
        whole = whole + ky_r[i].astype(F32)
    kout[pl.ds(x, 1)] = (
        dot(permo[...], whole.astype(BF16).reshape(slots, qcols)).astype(BF16)[None]
    )
    r_ko = []
    for d in range(1, NX):
        r_ko.append(remote(kout.at[x], kout.at[x], {"tensor": h * NX + lax.rem(x + d, NX)}))

    recv(r_gyx)
    for i in range(1, NY):
        acc = acc + gy_r[i].astype(F32)
    acc = acc * factor
    low, high = acc[: acc.shape[0] // 2], acc[acc.shape[0] // 2 :]
    gc_s[...] = jnp.where(c == 0, high, low)
    r_gcx = remote(gc_s, gout.at[c], partner)
    gout[pl.ds(c, 1)] = jnp.where(c == 0, low, high)[None]

    r_gc.wait_recv()
    outs = [local(gcb.at[i], gg_out.at[:, i * half : (i + 1) * half]) for i in range(2)]
    r_gcx.wait_recv()
    outs += [local(gout.at[i], gw_out.at[:, i * half : (i + 1) * half]) for i in range(2)]
    recv(r_ko)
    outs += [
        local(kout.at[q], keys_out.at[0, :, q * qcols : (q + 1) * qcols]) for q in range(NX)
    ]
    for d in sends:
        d.wait_send()
    for d in outs:
        d.wait()


def write_out(k_in, gw_in, gg_in, k_out, gw_out, gg_out, sem):
    pairs = ((k_in, k_out), (gw_in, gw_out), (gg_in, gg_out))
    copies = [pltpu.make_async_copy(a, b, sem.at[i]) for i, (a, b) in enumerate(pairs)]
    for d in copies:
        d.start()
    for d in copies:
        d.wait()


def build(mesh, dims):
    NY, NZ, NH, NX = dims
    LA, LB = NZ // 2, NZ // 2 - 1

    def on_device(hidden_rows, norm_gain, key_weight, cotangent, accepted_counts, destination):
        rows, cols = hidden_rows.shape
        half = cols // 2
        kvw = cotangent.shape[2]
        slots = 2 * rows
        kr = key_weight.shape[0]
        qcols = kvw // NX
        factor = 1.0 / math.sqrt(rows * lax.axis_size("dp"))
        V = pltpu.VMEM
        ncopies = 200
        scratch = [
            V((rows, cols), BF16),
            V((kr, cols), BF16),
            V((2, rows, half), BF16),
            V((NY, NZ, 2, kr, half), BF16),
            V((slots, slots), BF16),
            V((slots, slots), BF16),
            V((rows, slots), BF16),
            V((slots, rows), BF16),
            V((slots, kvw), BF16),
            V((NZ, 4 * NY, kvw), BF16),
            V((NZ, 4 * NY, kvw), BF16),
            V((2 * NY, 2 * NZ, kvw), BF16),
            V((2 * NY, 2 * NZ, kvw), BF16),
            V((2, rows, kvw), BF16),
            V((NH * NX, 1, rows), F32),
            V((2, 1, rows), F32),
            V((2 * rows, half), BF16),
            V((NY, NZ, 2 * kr, half), F32),
            V((NY, NZ, 2 * kr, half), BF16),
            V((NY, 2 * kr, half), BF16),
            V((LB, NY, 2 * kr, half), BF16),
            V((LB, NY, 2 * kr, half), BF16),
            V((max(LB - 1, 1), NY, 2 * kr, half), BF16),
            V((max(LB - 1, 1), NY, 2 * kr, half), BF16),
            V((NY, 2 * kr, half), BF16),
            V((NY, 2 * kr, half), BF16),
            V((kr, half), F32),
            V((2, kr, half), F32),
            V((NZ, 1, half), F32),
            V((NY, 1, half), F32),
            V((2, 1, half), F32),
            V((NX, 2, rows, qcols), BF16),
            V((NX, 2, rows, qcols), BF16),
            V((NZ, 4 * NY, qcols), BF16),
            V((NZ, 4 * NY, qcols), BF16),
            V((2 * NY, 2 * NZ, qcols), BF16),
            V((NH, 2 * NY, 2 * NZ, qcols), BF16),
            V((NX, slots, qcols), BF16),
            pltpu.SemaphoreType.DMA((ncopies,)),
            pltpu.SemaphoreType.DMA((ncopies,)),
            pltpu.SemaphoreType.DMA((16,)),
        ]
        any_spec = pl.BlockSpec(memory_space=pl.ANY)
        vmem = pl.BlockSpec(memory_space=pltpu.VMEM)
        keys, gw, gg = pl.pallas_call(
            functools.partial(kernel, dims, factor),
            out_shape=(
                V((1, slots, kvw), BF16),
                V((kr, cols), F32),
                V((1, cols), F32),
            ),
            in_specs=[any_spec, vmem, any_spec, any_spec, vmem, vmem],
            out_specs=(vmem, vmem, vmem),
            scratch_shapes=scratch,
            compiler_params=pltpu.CompilerParams(collective_id=0, has_side_effects=True),
            name="exchange",
        )(
            hidden_rows,
            norm_gain.reshape(1, cols),
            key_weight,
            cotangent,
            accepted_counts.reshape(1, 1),
            destination.reshape(1, rows),
        )
        keys, gw, gg = (
            pltpu.with_memory_space_constraint(a, pltpu.VMEM) for a in (keys, gw, gg)
        )
        keys, gw, gg = pl.pallas_call(
            write_out,
            out_shape=tuple(jax.ShapeDtypeStruct(a.shape, a.dtype) for a in (keys, gw, gg)),
            in_specs=[vmem] * 3,
            out_specs=(any_spec,) * 3,
            scratch_shapes=[pltpu.SemaphoreType.DMA((3,))],
            name="results",
        )(keys, gw, gg)
        return keys, gw, gg.reshape(cols)

    return jax.shard_map(
        on_device,
        mesh=mesh,
        in_specs=(
            P("dp", "tensor"),
            P("tensor"),
            P("dp", "tensor"),
            P("dp", None, None),
            P("dp"),
            P("dp"),
        ),
        out_specs=(P("dp", None, None), P("dp", "tensor"), P("tensor")),
        check_vma=False,
    )


def solution(mesh):
    return build(mesh, (4, 8, 2, 4))
```

```python
import functools
import math

import jax
import jax.numpy as jnp
from jax import lax
from jax.experimental import pallas as pl
from jax.experimental.pallas import tpu as pltpu
from jax.sharding import PartitionSpec as P

EPSILON = 1e-05
F32 = jnp.float32
BF16 = jnp.bfloat16
MESH = pl.DeviceIdType.MESH


def iota(shape, dim):
    return lax.broadcasted_iota(jnp.int32, shape, dim)


def onehot(cond):
    return jnp.where(cond, 1.0, 0.0).astype(BF16)


def kernel(
    dims,
    factor,
    hid,
    gain_ref,
    wsh,
    cot,
    count_ref,
    dest_ref,
    keys_out,
    gw_out,
    gg_out,
    hown,
    wown,
    hbuf,
    wall,
    permz,
    permo,
    pick,
    place,
    cotv,
    cot_a,
    cot_b1,
    cot_s,
    cot_b2,
    cot_r,
    sqb,
    sqc,
    norm,
    gf,
    gs,
    rj,
    ra,
    rb,
    sa,
    sb,
    gy_s,
    gy_r,
    gc_s,
    gout,
    gz,
    gyb,
    gcb,
    kx_s,
    kx_r,
    kz_s,
    kz_r,
    ky_s,
    ky_r,
    kout,
    ssem,
    rsem,
    lsem,
):
    NY, NZ, NH, NX = dims
    NT = NH * NX
    dp = lax.axis_index("dp")
    t = lax.axis_index("tensor")
    c = lax.rem(dp, 2)
    z = lax.rem(lax.div(dp, 2), NZ)
    y = lax.div(dp, 2 * NZ)
    x = lax.rem(t, NX)
    h = lax.div(t, NX)
    rows = dest_ref.shape[1]
    slots = 2 * rows
    half = hbuf.shape[2]
    width = half * 2 * NT
    kvw = cotv.shape[1]
    qcols = kvw // NX
    sign = 1 - 2 * c
    LA, LB = NZ // 2, NZ // 2 - 1

    def at_dp(yy, zz, cc):
        return {"dp": (yy * NZ + zz) * 2 + cc}

    partner = at_dp(y, z, 1 - c)
    z_fwd = at_dp(y, lax.rem(z + sign + NZ, NZ), c)
    z_bwd = at_dp(y, lax.rem(z - sign + NZ, NZ), c)
    z_jump = at_dp(y, lax.rem(z + 2 * sign + NZ, NZ), c)

    def zmod(v):
        return lax.rem(v + 2 * NZ, NZ)

    counter = [0]
    sends = []

    def remote(src, dst, dev):
        i = counter[0]
        counter[0] += 1
        d = pltpu.make_async_remote_copy(
            src_ref=src,
            dst_ref=dst,
            send_sem=ssem.at[i],
            recv_sem=rsem.at[i],
            device_id=dev,
            device_id_type=MESH,
        )
        d.start()
        sends.append(d)
        return d

    lcount = [0]

    def local(src, dst):
        i = lcount[0]
        lcount[0] += 1
        d = pltpu.make_async_copy(src, dst, lsem.at[i])
        d.start()
        return d

    own_cols = pl.ds(pl.multiple_of(c * half, half), half)
    other_cols = pl.ds(pl.multiple_of((1 - c) * half, half), half)

    barrier = pltpu.get_barrier_semaphore()
    peers = []
    for d in range(1, NZ):
        peers.append(at_dp(y, lax.rem(z + d, NZ), c))
    for dy in range(NY):
        for dc in range(2):
            if dy or dc:
                peers.append(at_dp(lax.rem(y + dy, NY), z, lax.rem(c + dc, 2)))
    for d in range(1, NT):
        peers.append({"tensor": lax.rem(t + d, NT)})
    for d in range(1, NX):
        peers.append(dict(at_dp(y, z, 1 - c), tensor=h * NX + lax.rem(x + d, NX)))
    for dy in range(NY):
        for dc in range(2):
            for dh in range(1, NH):
                if dy or dc:
                    peers.append(
                        dict(
                            at_dp(lax.rem(y + dy, NY), z, lax.rem(c + dc, 2)),
                            tensor=lax.rem(h + dh, NH) * NX + x,
                        )
                    )
    for p in peers:
        pl.semaphore_signal(barrier, inc=1, device_id=p, device_id_type=MESH)

    l_cot = local(cot.at[0], cotv)
    l_own = local(hid, hown)
    l_wv = local(wsh, wown)
    l_w = local(wsh.at[:, own_cols], wall.at[y, z, c])
    l_h = local(hid.at[:, own_cols], hbuf.at[c])

    def perm_zy():
        b = iota((slots, slots), 1)
        bz = (b // 4) % NZ
        by = b // (4 * NZ)
        return onehot(iota((slots, slots), 0) == bz * (4 * NY) + by * 4 + b % 4)

    def perm_yz():
        b = iota((slots, slots), 1)
        bz = b // (4 * NY)
        byc = (b // 2) % (2 * NY)
        return onehot(iota((slots, slots), 0) == byc * (2 * NZ) + bz * 2 + b % 2)

    def perm_out():
        b = iota((slots, slots), 1)
        by = b // (4 * NZ)
        bc = (b // (2 * NZ)) % 2
        bz = (b // 2) % NZ
        return onehot(iota((slots, slots), 0) == by * (4 * NZ) + bz * 4 + bc * 2 + b % 2)

    def dot(a, b):
        return jnp.dot(a, b, preferred_element_type=F32)

    l_cot.wait()
    mixed = dot(perm_zy(), cotv[...]).astype(BF16)
    cot_a[...] = mixed.reshape(NZ, 4 * NY, kvw)

    l_own.wait()
    eye = iota((rows, rows), 0) == iota((rows, rows), 1)

    def as_row(col):
        return jnp.sum(jnp.where(eye, col, 0.0), axis=0, keepdims=True)

    def as_col(row):
        return jnp.sum(jnp.where(eye, row, 0.0), axis=1, keepdims=True)

    values = hown[...].astype(F32)
    sqb[pl.ds(t, 1)] = as_row(jnp.sum(values * values, axis=1, keepdims=True))[None]

    permz[...] = perm_yz()
    permo[...] = perm_out()
    drow = dest_ref[...]
    dcol = as_col(drow.astype(F32)).astype(jnp.int32)
    same = dcol == drow
    rank_col = jnp.sum(
        jnp.where(same & (iota((rows, rows), 1) < iota((rows, rows), 0)), 1.0, 0.0),
        axis=1,
        keepdims=True,
    ).astype(jnp.int32)
    rank_row = jnp.sum(
        jnp.where(same & (iota((rows, rows), 0) < iota((rows, rows), 1)), 1.0, 0.0),
        axis=0,
        keepdims=True,
    ).astype(jnp.int32)
    count = count_ref[...].reshape(1, 1)

    def yc_of(dest):
        return (dest // (2 * NZ)) * 2 + dest % 2

    def z_of(dest):
        return (dest // 2) % NZ

    pos_col = yc_of(dcol) * (2 * NZ) + z_of(dcol) * 2 + rank_col
    pick[...] = onehot((iota((rows, slots), 1) == pos_col) & (iota((rows, slots), 0) < count))
    pos_row = z_of(drow) * (4 * NY) + yc_of(drow) * 2 + rank_row
    place[...] = onehot((iota((slots, rows), 0) == pos_row) & (iota((slots, rows), 1) < count))

    l_wv.wait()
    pl.semaphore_wait(barrier, len(peers))

    r_wy = {}
    for d in range(NY):
        for dc in range(2):
            if d or dc:
                cc = lax.rem(c + dc, 2)
                r_wy[d, dc] = remote(
                    wown.at[:, other_cols if dc else own_cols],
                    wall.at[y, z, c],
                    at_dp(lax.rem(y + d, NY), z, cc),
                )

    def z_exchange(src, dst):
        return [
            remote(src.at[lax.rem(z + d, NZ)], dst.at[z], at_dp(y, lax.rem(z + d, NZ), c))
            for d in range(1, NZ)
        ]

    def yc_exchange(src, dst):
        out = []
        for dy in range(NY):
            for dc in range(2):
                if dy or dc:
                    yy, cc = lax.rem(y + dy, NY), lax.rem(c + dc, 2)
                    out.append(remote(src.at[yy * 2 + cc], dst.at[y * 2 + c], at_dp(yy, z, cc)))
        return out

    def recv(copies):
        for d in copies:
            d.wait_recv()

    r_cz = z_exchange(cot_a, cot_b1)
    cot_b1[pl.ds(z, 1)] = cot_a[pl.ds(z, 1)]
    r_sq = [
        remote(sqb.at[t], sqb.at[t], {"tensor": lax.rem(t + d, NT)}) for d in range(1, NT)
    ]
    r_h = remote(hown.at[:, other_cols], hbuf.at[c], partner)

    def w_send(step, d, fwd, to):
        yy = lax.rem(y - d + NY, NY)
        zz = zmod(z - (step - 1) * sign) if fwd else zmod(z + (step - 1) * sign)
        return remote(wall.at[yy, zz], wall.at[yy, zz], to)

    w_got = {}

    def w_take(step, d, i):
        if (step, d) in w_got:
            w_got[step, d].pop(i).wait_recv()

    def w_step(step, d):
        if step <= LB:
            w_take(step - 1, d, 0)
            if step == LB:
                w_got[LA, d] = [w_send(step, d, True, z_jump)]
            w_got[step, d] = [w_send(step, d, True, z_fwd)]
        if step <= LB:
            w_take(step - 1, d, 0)
            w_got[step, d].append(w_send(step, d, False, z_bwd))

    def w_recv(step, d):
        for r in w_got.pop((step, d), ()):
            r.wait_recv()

    l_w.wait()
    r_wy[0, 1].wait_recv()
    w_step(1, 0)
    for d in range(1, NY):
        r_wy[d, 0].wait_recv()
        r_wy[d, 1].wait_recv()
        w_step(1, d)

    w_step(2, 0)

    recv(r_cz)
    cot_s[...] = (
        dot(permz[...], cot_b1[...].reshape(slots, kvw)).astype(BF16).reshape(2 * NY, 2 * NZ, kvw)
    )
    r_cy = yc_exchange(cot_s, cot_b2)
    cot_b2[pl.ds(y * 2 + c, 1)] = cot_s[pl.ds(y * 2 + c, 1)]

    for d in range(1, NY):
        w_step(2, d)

    recv(r_sq)
    total = sqb[0]
    for i in range(1, NT):
        total = total + sqb[i]
    sqc[pl.ds(c, 1)] = total[None]
    r_sc = remote(sqc.at[c], sqc.at[c], partner)

    for d in range(NY):
        w_step(3, d)

    recv(r_cy)
    cot_r[pl.ds(c, 1)] = dot(pick[...], cot_b2[...].reshape(slots, kvw)).astype(BF16)[None]
    r_cr = remote(cot_r.at[c], cot_r.at[c], partner)

    l_h.wait()
    r_h.wait_recv()
    r_sc.wait_recv()
    gain_half = gain_ref[:, own_cols]
    for i in range(2):
        scale = as_col(lax.rsqrt(sqc[i] / width + EPSILON))
        norm[i * rows : (i + 1) * rows] = (hbuf[i].astype(F32) * scale * gain_half).astype(BF16)

    r_cr.wait_recv()
    cot2 = cot_r[...].reshape(2 * rows, kvw)
    kb = kvw // NY
    for yy in range(NY):
        part = lax.dot_general(
            cot2[:, yy * kb : (yy + 1) * kb],
            norm[...],
            (((0,), (0,)), ((), ())),
            preferred_element_type=F32,
        ).reshape(NZ, kb // NZ, half)
        gf[yy] = part
        gs[yy] = part.astype(BF16)

    ga, gb, gj = {}, {}, {}
    order = list(range(1, NY)) + [0]

    def y_of(j):
        return lax.rem(y + j, NY)

    def own_g(j, zz):
        return gf[pl.ds(y_of(j), 1), pl.ds(zz, 1)][0, 0]

    for j in order:
        ga[1, j] = remote(gs.at[y_of(j), zmod(z + LB * sign)], ra.at[0, j], z_fwd)
        gb[1, j] = remote(gs.at[y_of(j), zmod(z - LB * sign)], rb.at[0, j], z_bwd)
        gj[j] = remote(gs.at[y_of(j), zmod(z + LA * sign)], rj.at[j], z_jump)

    def g_step(step):
        if step > LB:
            return
        for j in order:
            ga[step - 1, j].wait_recv()
            acc = ra[step - 2, j].astype(F32) + own_g(j, zmod(z + (LA - step) * sign))
            if step == 2:
                gj[j].wait_recv()
                acc = acc + rj[j].astype(F32)
            sa[step - 2, j] = acc.astype(BF16)
            ga[step, j] = remote(sa.at[step - 2, j], ra.at[step - 1, j], z_fwd)
            gb[step - 1, j].wait_recv()
            acc = rb[step - 2, j].astype(F32) + own_g(j, zmod(z - (LA - step) * sign))
            sb[step - 2, j] = acc.astype(BF16)
            gb[step, j] = remote(sb.at[step - 2, j], rb.at[step - 1, j], z_bwd)

    for d in range(NY):
        for step in range(1, LA + 1):
            w_recv(step, d)
        yy = lax.rem(y - d + NY, NY)
        block = lax.dot_general(
            norm[...],
            wall[pl.ds(yy, 1)].reshape(kb, half),
            (((1,), (1,)), ((), ())),
            preferred_element_type=F32,
        )
        kx_s[pl.ds(yy, 1)] = block.astype(BF16).reshape(1, 2, rows, qcols)
    r_kx = []
    for dc in range(2):
        for d in range(NX):
            if d or dc:
                xx, cc = lax.rem(x + d, NX), lax.rem(c + dc, 2)
                r_kx.append(
                    remote(
                        kx_s.at[xx, cc],
                        kx_r.at[x, c],
                        dict(at_dp(y, z, cc), tensor=h * NX + xx),
                    )
                )
    kx_r[pl.ds(x, 1), pl.ds(c, 1)] = kx_s[pl.ds(x, 1), pl.ds(c, 1)]

    gain_sum = jnp.zeros((1, half), F32)
    for yy in range(NY):
        gain_sum += jnp.sum(
            gf[yy].reshape(kb, half) * wall[yy].reshape(kb, half).astype(F32), axis=0, keepdims=True
        )
    gz[pl.ds(z, 1)] = gain_sum[None]
    r_gz = [
        remote(gz.at[z], gz.at[z], at_dp(y, lax.rem(z + d, NZ), c)) for d in range(1, NZ)
    ]

    recv(r_kx)
    mine_k = kx_r[0, 0].astype(F32)
    for i in range(1, 2 * NX):
        mine_k = mine_k + kx_r[i // 2, i % 2].astype(F32)
    kz_s[...] = dot(place[...], mine_k.astype(BF16)).astype(BF16).reshape(NZ, 4 * NY, qcols)
    r_kz = z_exchange(kz_s, kz_r)
    kz_r[pl.ds(z, 1)] = kz_s[pl.ds(z, 1)]

    g_step(2)

    recv(r_gz)
    gain_sum = gz[0]
    for i in range(1, NZ):
        gain_sum = gain_sum + gz[i]
    gyb[pl.ds(y, 1)] = gain_sum[None]
    r_gy = [
        remote(gyb.at[y], gyb.at[y], at_dp(lax.rem(y + d, NY), z, c)) for d in range(1, NY)
    ]

    recv(r_kz)
    ky_s[...] = (
        dot(permz[...], kz_r[...].reshape(slots, qcols)).astype(BF16).reshape(2 * NY, 2 * NZ, qcols)
    )
    r_ky = []
    for dh in range(NH):
        for dy in range(NY):
            for dc in range(2):
                if dy or dc or dh:
                    yy, cc, hh = lax.rem(y + dy, NY), lax.rem(c + dc, 2), lax.rem(h + dh, NH)
                    r_ky.append(
                        remote(
                            ky_s.at[yy * 2 + cc],
                            ky_r.at[h, y * 2 + c],
                            dict(at_dp(yy, z, cc), tensor=hh * NX + x),
                        )
                    )
    ky_r[pl.ds(h, 1), pl.ds(y * 2 + c, 1)] = ky_s[pl.ds(y * 2 + c, 1)][None]

    g_step(3)

    recv(r_gy)
    gain_sum = gyb[0]
    for i in range(1, NY):
        gain_sum = gain_sum + gyb[i]
    gcb[pl.ds(c, 1)] = (gain_sum * factor / gain_half)[None]
    r_gc = remote(gcb.at[c], gcb.at[c], partner)

    r_gyx = []
    for j in order:
        ga[LB, j].wait_recv()
        gb[LB, j].wait_recv()
        acc = own_g(j, z) + ra[LB - 1, j].astype(F32) + rb[LB - 1, j].astype(F32)
        if LB == 1:
            gj[j].wait_recv()
            acc = acc + rj[j].astype(F32)
        if j:
            gy_s[j] = acc.astype(BF16)
            r_gyx.append(remote(gy_s.at[j], gy_r.at[j], at_dp(y_of(j), z, c)))

    recv(r_ky)
    whole = ky_r[0].astype(F32)
    for i in range(1, NH):
        whole = whole + ky_r[i].astype(F32)
    kout[pl.ds(x, 1)] = (
        dot(permo[...], whole.astype(BF16).reshape(slots, qcols)).astype(BF16)[None]
    )
    r_ko = []
    for d in range(1, NX):
        r_ko.append(remote(kout.at[x], kout.at[x], {"tensor": h * NX + lax.rem(x + d, NX)}))

    recv(r_gyx)
    for i in range(1, NY):
        acc = acc + gy_r[i].astype(F32)
    acc = acc * factor
    low, high = acc[: acc.shape[0] // 2], acc[acc.shape[0] // 2 :]
    gc_s[...] = jnp.where(c == 0, high, low)
    r_gcx = remote(gc_s, gout.at[c], partner)
    gout[pl.ds(c, 1)] = jnp.where(c == 0, low, high)[None]

    r_gc.wait_recv()
    outs = [local(gcb.at[i], gg_out.at[:, i * half : (i + 1) * half]) for i in range(2)]
    r_gcx.wait_recv()
    outs += [local(gout.at[i], gw_out.at[:, i * half : (i + 1) * half]) for i in range(2)]
    recv(r_ko)
    outs += [
        local(kout.at[q], keys_out.at[0, :, q * qcols : (q + 1) * qcols]) for q in range(NX)
    ]
    for d in sends:
        d.wait_send()
    for d in outs:
        d.wait()


def write_out(k_in, gw_in, gg_in, k_out, gw_out, gg_out, sem):
    pairs = ((k_in, k_out), (gw_in, gw_out), (gg_in, gg_out))
    copies = [pltpu.make_async_copy(a, b, sem.at[i]) for i, (a, b) in enumerate(pairs)]
    for d in copies:
        d.start()
    for d in copies:
        d.wait()


def build(mesh, dims):
    NY, NZ, NH, NX = dims
    LA, LB = NZ // 2, NZ // 2 - 1

    def on_device(hidden_rows, norm_gain, key_weight, cotangent, accepted_counts, destination):
        rows, cols = hidden_rows.shape
        half = cols // 2
        kvw = cotangent.shape[2]
        slots = 2 * rows
        kr = key_weight.shape[0]
        qcols = kvw // NX
        factor = 1.0 / math.sqrt(rows * lax.axis_size("dp"))
        V = pltpu.VMEM
        ncopies = 200
        scratch = [
            V((rows, cols), BF16),
            V((kr, cols), BF16),
            V((2, rows, half), BF16),
            V((NY, NZ, 2, kr, half), BF16),
            V((slots, slots), BF16),
            V((slots, slots), BF16),
            V((rows, slots), BF16),
            V((slots, rows), BF16),
            V((slots, kvw), BF16),
            V((NZ, 4 * NY, kvw), BF16),
            V((NZ, 4 * NY, kvw), BF16),
            V((2 * NY, 2 * NZ, kvw), BF16),
            V((2 * NY, 2 * NZ, kvw), BF16),
            V((2, rows, kvw), BF16),
            V((NH * NX, 1, rows), F32),
            V((2, 1, rows), F32),
            V((2 * rows, half), BF16),
            V((NY, NZ, 2 * kr, half), F32),
            V((NY, NZ, 2 * kr, half), BF16),
            V((NY, 2 * kr, half), BF16),
            V((LB, NY, 2 * kr, half), BF16),
            V((LB, NY, 2 * kr, half), BF16),
            V((max(LB - 1, 1), NY, 2 * kr, half), BF16),
            V((max(LB - 1, 1), NY, 2 * kr, half), BF16),
            V((NY, 2 * kr, half), BF16),
            V((NY, 2 * kr, half), BF16),
            V((kr, half), F32),
            V((2, kr, half), F32),
            V((NZ, 1, half), F32),
            V((NY, 1, half), F32),
            V((2, 1, half), F32),
            V((NX, 2, rows, qcols), BF16),
            V((NX, 2, rows, qcols), BF16),
            V((NZ, 4 * NY, qcols), BF16),
            V((NZ, 4 * NY, qcols), BF16),
            V((2 * NY, 2 * NZ, qcols), BF16),
            V((NH, 2 * NY, 2 * NZ, qcols), BF16),
            V((NX, slots, qcols), BF16),
            pltpu.SemaphoreType.DMA((ncopies,)),
            pltpu.SemaphoreType.DMA((ncopies,)),
            pltpu.SemaphoreType.DMA((16,)),
        ]
        any_spec = pl.BlockSpec(memory_space=pl.ANY)
        vmem = pl.BlockSpec(memory_space=pltpu.VMEM)
        keys, gw, gg = pl.pallas_call(
            functools.partial(kernel, dims, factor),
            out_shape=(
                V((1, slots, kvw), BF16),
                V((kr, cols), F32),
                V((1, cols), F32),
            ),
            in_specs=[any_spec, vmem, any_spec, any_spec, vmem, vmem],
            out_specs=(vmem, vmem, vmem),
            scratch_shapes=scratch,
            compiler_params=pltpu.CompilerParams(collective_id=0, has_side_effects=True),
            name="exchange",
        )(
            hidden_rows,
            norm_gain.reshape(1, cols),
            key_weight,
            cotangent,
            accepted_counts,
            destination.reshape(1, rows),
        )
        keys, gw, gg = (
            pltpu.with_memory_space_constraint(a, pltpu.VMEM) for a in (keys, gw, gg)
        )
        keys, gw, gg = pl.pallas_call(
            write_out,
            out_shape=tuple(jax.ShapeDtypeStruct(a.shape, a.dtype) for a in (keys, gw, gg)),
            in_specs=[vmem] * 3,
            out_specs=(any_spec,) * 3,
            scratch_shapes=[pltpu.SemaphoreType.DMA((3,))],
            name="results",
        )(keys, gw, gg)
        return keys, gw, gg.reshape(cols)

    return jax.shard_map(
        on_device,
        mesh=mesh,
        in_specs=(
            P("dp", "tensor"),
            P("tensor"),
            P("dp", "tensor"),
            P("dp", None, None),
            P("dp"),
            P("dp"),
        ),
        out_specs=(P("dp", None, None), P("dp", "tensor"), P("tensor")),
        check_vma=False,
    )


def solution(mesh):
    return build(mesh, (4, 8, 2, 4))
```

```python
import functools
import math

import jax
import jax.numpy as jnp
from jax import lax
from jax.experimental import pallas as pl
from jax.experimental.pallas import tpu as pltpu
from jax.sharding import PartitionSpec as P

EPSILON = 1e-05
F32 = jnp.float32
BF16 = jnp.bfloat16
MESH = pl.DeviceIdType.MESH


def iota(shape, dim):
    return lax.broadcasted_iota(jnp.int32, shape, dim)


def onehot(cond):
    return jnp.where(cond, 1.0, 0.0).astype(BF16)


def kernel(
    dims,
    factor,
    hid,
    gain_ref,
    wsh,
    cot,
    count_ref,
    dest_ref,
    keys_out,
    gw_out,
    gg_out,
    hown,
    wown,
    hbuf,
    wall,
    permz,
    permo,
    pick,
    place,
    cotv,
    cot_a,
    cot_b1,
    cot_s,
    cot_b2,
    cot_r,
    sqb,
    sqc,
    norm,
    gf,
    gs,
    rj,
    ra,
    rb,
    sa,
    sb,
    gy_s,
    gy_r,
    gc_s,
    gout,
    gz,
    gyb,
    gcb,
    kx_s,
    kx_r,
    kz_s,
    kz_r,
    ky_s,
    ky_r,
    kout,
    ssem,
    rsem,
    lsem,
):
    NY, NZ, NH, NX = dims
    NT = NH * NX
    dp = lax.axis_index("dp")
    t = lax.axis_index("tensor")
    c = lax.rem(dp, 2)
    z = lax.rem(lax.div(dp, 2), NZ)
    y = lax.div(dp, 2 * NZ)
    x = lax.rem(t, NX)
    h = lax.div(t, NX)
    rows = dest_ref.shape[1]
    slots = 2 * rows
    half = hbuf.shape[2]
    width = half * 2 * NT
    kvw = cotv.shape[1]
    qcols = kvw // NX
    sign = 1 - 2 * c
    LA, LB = NZ // 2, NZ // 2 - 1

    def at_dp(yy, zz, cc):
        return {"dp": (yy * NZ + zz) * 2 + cc}

    partner = at_dp(y, z, 1 - c)
    z_fwd = at_dp(y, lax.rem(z + sign + NZ, NZ), c)
    z_bwd = at_dp(y, lax.rem(z - sign + NZ, NZ), c)
    z_jump = at_dp(y, lax.rem(z + 2 * sign + NZ, NZ), c)

    def y_pair(d):
        v = y
        for bit in (1, 2):
            if d & bit:
                v = v + bit - 2 * bit * lax.rem(lax.div(y, bit), 2)
        return v

    def zmod(v):
        return lax.rem(v + 2 * NZ, NZ)

    counter = [0]
    sends = []

    def remote(src, dst, dev):
        i = counter[0]
        counter[0] += 1
        d = pltpu.make_async_remote_copy(
            src_ref=src,
            dst_ref=dst,
            send_sem=ssem.at[i],
            recv_sem=rsem.at[i],
            device_id=dev,
            device_id_type=MESH,
        )
        d.start()
        sends.append(d)
        return d

    lcount = [0]

    def local(src, dst):
        i = lcount[0]
        lcount[0] += 1
        d = pltpu.make_async_copy(src, dst, lsem.at[i])
        d.start()
        return d

    own_cols = pl.ds(pl.multiple_of(c * half, half), half)
    other_cols = pl.ds(pl.multiple_of((1 - c) * half, half), half)

    barrier = pltpu.get_barrier_semaphore()
    peers = []
    for d in range(1, NZ):
        peers.append(at_dp(y, lax.rem(z + d, NZ), c))
    for dy in range(NY):
        for dc in range(2):
            if dy or dc:
                peers.append(at_dp(lax.rem(y + dy, NY), z, lax.rem(c + dc, 2)))
    for d in range(1, NT):
        peers.append({"tensor": lax.rem(t + d, NT)})
    for d in range(1, NX):
        peers.append(dict(at_dp(y, z, 1 - c), tensor=h * NX + lax.rem(x + d, NX)))
    for dy in range(NY):
        for dc in range(2):
            for dh in range(1, NH):
                if dy or dc:
                    peers.append(
                        dict(
                            at_dp(lax.rem(y + dy, NY), z, lax.rem(c + dc, 2)),
                            tensor=lax.rem(h + dh, NH) * NX + x,
                        )
                    )
    for p in peers:
        pl.semaphore_signal(barrier, inc=1, device_id=p, device_id_type=MESH)

    l_cot = local(cot.at[0], cotv)
    l_own = local(hid, hown)
    l_wv = local(wsh, wown)
    l_w = local(wsh.at[:, own_cols], wall.at[y, z, c])
    l_h = local(hid.at[:, own_cols], hbuf.at[c])

    def perm_zy():
        b = iota((slots, slots), 1)
        bz = (b // 4) % NZ
        by = b // (4 * NZ)
        return onehot(iota((slots, slots), 0) == bz * (4 * NY) + by * 4 + b % 4)

    def perm_yz():
        b = iota((slots, slots), 1)
        bz = b // (4 * NY)
        byc = (b // 2) % (2 * NY)
        return onehot(iota((slots, slots), 0) == byc * (2 * NZ) + bz * 2 + b % 2)

    def perm_out():
        b = iota((slots, slots), 1)
        by = b // (4 * NZ)
        bc = (b // (2 * NZ)) % 2
        bz = (b // 2) % NZ
        return onehot(iota((slots, slots), 0) == by * (4 * NZ) + bz * 4 + bc * 2 + b % 2)

    def dot(a, b):
        return jnp.dot(a, b, preferred_element_type=F32)

    l_cot.wait()
    mixed = dot(perm_zy(), cotv[...]).astype(BF16)
    cot_a[...] = mixed.reshape(NZ, 4 * NY, kvw)

    l_own.wait()
    eye = iota((rows, rows), 0) == iota((rows, rows), 1)

    def as_row(col):
        return jnp.sum(jnp.where(eye, col, 0.0), axis=0, keepdims=True)

    def as_col(row):
        return jnp.sum(jnp.where(eye, row, 0.0), axis=1, keepdims=True)

    values = hown[...].astype(F32)
    sqb[pl.ds(t, 1)] = as_row(jnp.sum(values * values, axis=1, keepdims=True))[None]

    permz[...] = perm_yz()
    permo[...] = perm_out()
    drow = dest_ref[...]
    dcol = as_col(drow.astype(F32)).astype(jnp.int32)
    same = dcol == drow
    rank_col = jnp.sum(
        jnp.where(same & (iota((rows, rows), 1) < iota((rows, rows), 0)), 1.0, 0.0),
        axis=1,
        keepdims=True,
    ).astype(jnp.int32)
    rank_row = jnp.sum(
        jnp.where(same & (iota((rows, rows), 0) < iota((rows, rows), 1)), 1.0, 0.0),
        axis=0,
        keepdims=True,
    ).astype(jnp.int32)
    count = count_ref[...].reshape(1, 1)

    def yc_of(dest):
        return (dest // (2 * NZ)) * 2 + dest % 2

    def z_of(dest):
        return (dest // 2) % NZ

    pos_col = yc_of(dcol) * (2 * NZ) + z_of(dcol) * 2 + rank_col
    pick[...] = onehot((iota((rows, slots), 1) == pos_col) & (iota((rows, slots), 0) < count))
    pos_row = z_of(drow) * (4 * NY) + yc_of(drow) * 2 + rank_row
    place[...] = onehot((iota((slots, rows), 0) == pos_row) & (iota((slots, rows), 1) < count))

    l_wv.wait()
    pl.semaphore_wait(barrier, len(peers))

    r_wy = {}
    for d in range(NY):
        for dc in range(2):
            if d or dc:
                cc = lax.rem(c + dc, 2)
                r_wy[d, dc] = remote(
                    wown.at[:, other_cols if dc else own_cols],
                    wall.at[y, z, c],
                    at_dp(y_pair(d), z, cc),
                )

    def z_exchange(src, dst):
        return [
            remote(src.at[lax.rem(z + d, NZ)], dst.at[z], at_dp(y, lax.rem(z + d, NZ), c))
            for d in range(1, NZ)
        ]

    def yc_exchange(src, dst):
        out = []
        for dy in range(NY):
            for dc in range(2):
                if dy or dc:
                    yy, cc = lax.rem(y + dy, NY), lax.rem(c + dc, 2)
                    out.append(remote(src.at[yy * 2 + cc], dst.at[y * 2 + c], at_dp(yy, z, cc)))
        return out

    def recv(copies):
        for d in copies:
            d.wait_recv()

    r_cz = z_exchange(cot_a, cot_b1)
    cot_b1[pl.ds(z, 1)] = cot_a[pl.ds(z, 1)]
    r_sq = [
        remote(sqb.at[t], sqb.at[t], {"tensor": lax.rem(t + d, NT)}) for d in range(1, NT)
    ]
    r_h = remote(hown.at[:, other_cols], hbuf.at[c], partner)

    def w_send(step, d, fwd, to):
        yy = y_pair(d)
        zz = zmod(z - (step - 1) * sign) if fwd else zmod(z + (step - 1) * sign)
        return remote(wall.at[yy, zz], wall.at[yy, zz], to)

    w_got = {}

    def w_take(step, d, i):
        if (step, d) in w_got:
            w_got[step, d].pop(i).wait_recv()

    def w_step(step, d):
        if step <= LB:
            w_take(step - 1, d, 0)
            if step == LB:
                w_got[LA, d] = [w_send(step, d, True, z_jump)]
            w_got[step, d] = [w_send(step, d, True, z_fwd)]
        if step <= LB:
            w_take(step - 1, d, 0)
            w_got[step, d].append(w_send(step, d, False, z_bwd))

    def w_recv(step, d):
        for r in w_got.pop((step, d), ()):
            r.wait_recv()

    l_w.wait()
    r_wy[0, 1].wait_recv()
    w_step(1, 0)
    for d in range(1, NY):
        r_wy[d, 0].wait_recv()
        r_wy[d, 1].wait_recv()
        w_step(1, d)

    w_step(2, 0)

    recv(r_cz)
    cot_s[...] = (
        dot(permz[...], cot_b1[...].reshape(slots, kvw)).astype(BF16).reshape(2 * NY, 2 * NZ, kvw)
    )
    r_cy = yc_exchange(cot_s, cot_b2)
    cot_b2[pl.ds(y * 2 + c, 1)] = cot_s[pl.ds(y * 2 + c, 1)]

    for d in range(1, NY):
        w_step(2, d)

    recv(r_sq)
    total = sqb[0]
    for i in range(1, NT):
        total = total + sqb[i]
    sqc[pl.ds(c, 1)] = total[None]
    r_sc = remote(sqc.at[c], sqc.at[c], partner)

    for d in range(NY):
        w_step(3, d)

    recv(r_cy)
    cot_r[pl.ds(c, 1)] = dot(pick[...], cot_b2[...].reshape(slots, kvw)).astype(BF16)[None]
    r_cr = remote(cot_r.at[c], cot_r.at[c], partner)

    l_h.wait()
    r_h.wait_recv()
    r_sc.wait_recv()
    gain_half = gain_ref[:, own_cols]
    for i in range(2):
        scale = as_col(lax.rsqrt(sqc[i] / width + EPSILON))
        norm[i * rows : (i + 1) * rows] = (hbuf[i].astype(F32) * scale * gain_half).astype(BF16)

    r_cr.wait_recv()
    cot2 = cot_r[...].reshape(2 * rows, kvw)
    kb = kvw // NY
    for yy in range(NY):
        part = lax.dot_general(
            cot2[:, yy * kb : (yy + 1) * kb],
            norm[...],
            (((0,), (0,)), ((), ())),
            preferred_element_type=F32,
        ).reshape(NZ, kb // NZ, half)
        gf[yy] = part
        gs[yy] = part.astype(BF16)

    ga, gb, gj = {}, {}, {}
    order = list(range(1, NY)) + [0]

    def y_of(j):
        return lax.rem(y + j, NY)

    def own_g(j, zz):
        return gf[pl.ds(y_of(j), 1), pl.ds(zz, 1)][0, 0]

    for j in order:
        ga[1, j] = remote(gs.at[y_of(j), zmod(z + LB * sign)], ra.at[0, j], z_fwd)
        gb[1, j] = remote(gs.at[y_of(j), zmod(z - LB * sign)], rb.at[0, j], z_bwd)
        gj[j] = remote(gs.at[y_of(j), zmod(z + LA * sign)], rj.at[j], z_jump)

    def g_step(step):
        if step > LB:
            return
        for j in order:
            ga[step - 1, j].wait_recv()
            acc = ra[step - 2, j].astype(F32) + own_g(j, zmod(z + (LA - step) * sign))
            if step == 2:
                gj[j].wait_recv()
                acc = acc + rj[j].astype(F32)
            sa[step - 2, j] = acc.astype(BF16)
            ga[step, j] = remote(sa.at[step - 2, j], ra.at[step - 1, j], z_fwd)
            gb[step - 1, j].wait_recv()
            acc = rb[step - 2, j].astype(F32) + own_g(j, zmod(z - (LA - step) * sign))
            sb[step - 2, j] = acc.astype(BF16)
            gb[step, j] = remote(sb.at[step - 2, j], rb.at[step - 1, j], z_bwd)

    for d in range(NY):
        for step in range(1, LA + 1):
            w_recv(step, d)
        yy = y_pair(d)
        block = lax.dot_general(
            norm[...],
            wall[pl.ds(yy, 1)].reshape(kb, half),
            (((1,), (1,)), ((), ())),
            preferred_element_type=F32,
        )
        kx_s[pl.ds(yy, 1)] = block.astype(BF16).reshape(1, 2, rows, qcols)
    r_kx = []
    for dc in range(2):
        for d in range(NX):
            if d or dc:
                xx, cc = lax.rem(x + d, NX), lax.rem(c + dc, 2)
                r_kx.append(
                    remote(
                        kx_s.at[xx, cc],
                        kx_r.at[x, c],
                        dict(at_dp(y, z, cc), tensor=h * NX + xx),
                    )
                )
    kx_r[pl.ds(x, 1), pl.ds(c, 1)] = kx_s[pl.ds(x, 1), pl.ds(c, 1)]

    gain_sum = jnp.zeros((1, half), F32)
    for yy in range(NY):
        gain_sum += jnp.sum(
            gf[yy].reshape(kb, half) * wall[yy].reshape(kb, half).astype(F32), axis=0, keepdims=True
        )
    gz[pl.ds(z, 1)] = gain_sum[None]
    r_gz = [
        remote(gz.at[z], gz.at[z], at_dp(y, lax.rem(z + d, NZ), c)) for d in range(1, NZ)
    ]

    recv(r_kx)
    mine_k = kx_r[0, 0].astype(F32)
    for i in range(1, 2 * NX):
        mine_k = mine_k + kx_r[i // 2, i % 2].astype(F32)
    kz_s[...] = dot(place[...], mine_k.astype(BF16)).astype(BF16).reshape(NZ, 4 * NY, qcols)
    r_kz = z_exchange(kz_s, kz_r)
    kz_r[pl.ds(z, 1)] = kz_s[pl.ds(z, 1)]

    g_step(2)

    recv(r_gz)
    gain_sum = gz[0]
    for i in range(1, NZ):
        gain_sum = gain_sum + gz[i]
    gyb[pl.ds(y, 1)] = gain_sum[None]
    r_gy = [
        remote(gyb.at[y], gyb.at[y], at_dp(lax.rem(y + d, NY), z, c)) for d in range(1, NY)
    ]

    recv(r_kz)
    ky_s[...] = (
        dot(permz[...], kz_r[...].reshape(slots, qcols)).astype(BF16).reshape(2 * NY, 2 * NZ, qcols)
    )
    r_ky = []
    for dh in range(NH):
        for dy in range(NY):
            for dc in range(2):
                if dy or dc or dh:
                    yy, cc, hh = lax.rem(y + dy, NY), lax.rem(c + dc, 2), lax.rem(h + dh, NH)
                    r_ky.append(
                        remote(
                            ky_s.at[yy * 2 + cc],
                            ky_r.at[h, y * 2 + c],
                            dict(at_dp(yy, z, cc), tensor=hh * NX + x),
                        )
                    )
    ky_r[pl.ds(h, 1), pl.ds(y * 2 + c, 1)] = ky_s[pl.ds(y * 2 + c, 1)][None]

    g_step(3)

    recv(r_gy)
    gain_sum = gyb[0]
    for i in range(1, NY):
        gain_sum = gain_sum + gyb[i]
    gcb[pl.ds(c, 1)] = (gain_sum * factor / gain_half)[None]
    r_gc = remote(gcb.at[c], gcb.at[c], partner)

    r_gyx = []
    for j in order:
        ga[LB, j].wait_recv()
        gb[LB, j].wait_recv()
        acc = own_g(j, z) + ra[LB - 1, j].astype(F32) + rb[LB - 1, j].astype(F32)
        if LB == 1:
            gj[j].wait_recv()
            acc = acc + rj[j].astype(F32)
        if j:
            gy_s[j] = acc.astype(BF16)
            r_gyx.append(remote(gy_s.at[j], gy_r.at[j], at_dp(y_of(j), z, c)))

    recv(r_ky)
    whole = ky_r[0].astype(F32)
    for i in range(1, NH):
        whole = whole + ky_r[i].astype(F32)
    kout[pl.ds(x, 1)] = (
        dot(permo[...], whole.astype(BF16).reshape(slots, qcols)).astype(BF16)[None]
    )
    r_ko = []
    for d in range(1, NX):
        r_ko.append(remote(kout.at[x], kout.at[x], {"tensor": h * NX + lax.rem(x + d, NX)}))

    recv(r_gyx)
    for i in range(1, NY):
        acc = acc + gy_r[i].astype(F32)
    acc = acc * factor
    low, high = acc[: acc.shape[0] // 2], acc[acc.shape[0] // 2 :]
    gc_s[...] = jnp.where(c == 0, high, low)
    r_gcx = remote(gc_s, gout.at[c], partner)
    gout[pl.ds(c, 1)] = jnp.where(c == 0, low, high)[None]

    r_gc.wait_recv()
    outs = [local(gcb.at[i], gg_out.at[:, i * half : (i + 1) * half]) for i in range(2)]
    r_gcx.wait_recv()
    outs += [local(gout.at[i], gw_out.at[:, i * half : (i + 1) * half]) for i in range(2)]
    recv(r_ko)
    outs += [
        local(kout.at[q], keys_out.at[0, :, q * qcols : (q + 1) * qcols]) for q in range(NX)
    ]
    for d in sends:
        d.wait_send()
    for d in outs:
        d.wait()


def write_out(k_in, gw_in, gg_in, k_out, gw_out, gg_out, sem):
    pairs = ((k_in, k_out), (gw_in, gw_out), (gg_in, gg_out))
    copies = [pltpu.make_async_copy(a, b, sem.at[i]) for i, (a, b) in enumerate(pairs)]
    for d in copies:
        d.start()
    for d in copies:
        d.wait()


def build(mesh, dims):
    NY, NZ, NH, NX = dims
    LA, LB = NZ // 2, NZ // 2 - 1

    def on_device(hidden_rows, norm_gain, key_weight, cotangent, accepted_counts, destination):
        rows, cols = hidden_rows.shape
        half = cols // 2
        kvw = cotangent.shape[2]
        slots = 2 * rows
        kr = key_weight.shape[0]
        qcols = kvw // NX
        factor = 1.0 / math.sqrt(rows * lax.axis_size("dp"))
        V = pltpu.VMEM
        ncopies = 200
        scratch = [
            V((rows, cols), BF16),
            V((kr, cols), BF16),
            V((2, rows, half), BF16),
            V((NY, NZ, 2, kr, half), BF16),
            V((slots, slots), BF16),
            V((slots, slots), BF16),
            V((rows, slots), BF16),
            V((slots, rows), BF16),
            V((slots, kvw), BF16),
            V((NZ, 4 * NY, kvw), BF16),
            V((NZ, 4 * NY, kvw), BF16),
            V((2 * NY, 2 * NZ, kvw), BF16),
            V((2 * NY, 2 * NZ, kvw), BF16),
            V((2, rows, kvw), BF16),
            V((NH * NX, 1, rows), F32),
            V((2, 1, rows), F32),
            V((2 * rows, half), BF16),
            V((NY, NZ, 2 * kr, half), F32),
            V((NY, NZ, 2 * kr, half), BF16),
            V((NY, 2 * kr, half), BF16),
            V((LB, NY, 2 * kr, half), BF16),
            V((LB, NY, 2 * kr, half), BF16),
            V((max(LB - 1, 1), NY, 2 * kr, half), BF16),
            V((max(LB - 1, 1), NY, 2 * kr, half), BF16),
            V((NY, 2 * kr, half), BF16),
            V((NY, 2 * kr, half), BF16),
            V((kr, half), F32),
            V((2, kr, half), F32),
            V((NZ, 1, half), F32),
            V((NY, 1, half), F32),
            V((2, 1, half), F32),
            V((NX, 2, rows, qcols), BF16),
            V((NX, 2, rows, qcols), BF16),
            V((NZ, 4 * NY, qcols), BF16),
            V((NZ, 4 * NY, qcols), BF16),
            V((2 * NY, 2 * NZ, qcols), BF16),
            V((NH, 2 * NY, 2 * NZ, qcols), BF16),
            V((NX, slots, qcols), BF16),
            pltpu.SemaphoreType.DMA((ncopies,)),
            pltpu.SemaphoreType.DMA((ncopies,)),
            pltpu.SemaphoreType.DMA((16,)),
        ]
        any_spec = pl.BlockSpec(memory_space=pl.ANY)
        vmem = pl.BlockSpec(memory_space=pltpu.VMEM)
        keys, gw, gg = pl.pallas_call(
            functools.partial(kernel, dims, factor),
            out_shape=(
                V((1, slots, kvw), BF16),
                V((kr, cols), F32),
                V((1, cols), F32),
            ),
            in_specs=[any_spec, vmem, any_spec, any_spec, vmem, vmem],
            out_specs=(vmem, vmem, vmem),
            scratch_shapes=scratch,
            compiler_params=pltpu.CompilerParams(collective_id=0, has_side_effects=True),
            name="exchange",
        )(
            hidden_rows,
            norm_gain.reshape(1, cols),
            key_weight,
            cotangent,
            accepted_counts,
            destination.reshape(1, rows),
        )
        keys, gw, gg = (
            pltpu.with_memory_space_constraint(a, pltpu.VMEM) for a in (keys, gw, gg)
        )
        keys, gw, gg = pl.pallas_call(
            write_out,
            out_shape=tuple(jax.ShapeDtypeStruct(a.shape, a.dtype) for a in (keys, gw, gg)),
            in_specs=[vmem] * 3,
            out_specs=(any_spec,) * 3,
            scratch_shapes=[pltpu.SemaphoreType.DMA((3,))],
            name="results",
        )(keys, gw, gg)
        return keys, gw, gg.reshape(cols)

    return jax.shard_map(
        on_device,
        mesh=mesh,
        in_specs=(
            P("dp", "tensor"),
            P("tensor"),
            P("dp", "tensor"),
            P("dp", None, None),
            P("dp"),
            P("dp"),
        ),
        out_specs=(P("dp", None, None), P("dp", "tensor"), P("tensor")),
        check_vma=False,
    )


def solution(mesh):
    return build(mesh, (4, 8, 2, 4))
```
